512 devices in a mesh: dp: 32 (over z_lo, x), mp: 16 (over y, z_hi, core).
Axes of the slice: x: 4, y: 4, z: 16 (z_hi: 2, z_lo: 8; z = z_hi * 8 + z_lo), core: 2. Of those that a mesh axis runs over, the one named last changes fastest.
Arguments:
- patches: bfloat16 [8192, 6144], P('dp', 'mp')
- destination: int32 [8192], P('dp'), may hold values from 0 to 8191, as said below
- segment: int32 [8192], P('dp'), may hold values from 0 to 8191, as said below
- ln_gain: float32 [6144], replicated
- w_query: bfloat16 [6144, 4096], P('dp', 'mp')
- w_key: bfloat16 [6144, 4096], P('dp', 'mp')
- w_value: bfloat16 [6144, 4096], P('dp', 'mp')
- query_gain: float32 [4096], P('mp')
- key_gain: float32 [4096], P('mp')
- attn_cotangent: bfloat16 [8192, 4096], P('dp', 'mp'), may hold values from -6 to 6
Outputs:
- attention: bfloat16 [8192, 4096], P('dp', 'mp')
- grad_packed: bfloat16 [8192, 6144], P('dp', 'mp')
The draws below stay inside these ranges and needn't reach their ends.
Inputs may be any that keep to these rules, and one draw needn't show every extreme that they name: `destination`: each number appears once. The 256 loader rows of one index of dp place at most 16 rows into any one packed sequence, and exactly 16 into some sequence. `segment`: image ids never fall along the packed rows, and no image crosses the boundary between two packed sequences of 256 rows. Each image has 1 to min(64, 128) patches, and every packed sequence holds one image of exactly that most.
All inputs are finite; a program needn't handle non-finite values.
Results may differ from the reference program's by a relative error of at most 0.023.
The reference program's roundings to bfloat16 on the way (of `packed`, `normed`, `query_norm`, `prob_half`, `grad_score`, `value_grad` and `query_grad`) count: a program that leaves them out, or rounds other values in their place, can miss the bound.
Values may be sent and summed in bfloat16 or wider, within the bound.
No kernel may reach another device: no remote copies, remote signals or barrier semaphores. Data moves between devices by JAX's collectives and lax.ppermute only.
A program may use at most 64 MiB of HBM per device.

```python
import math
import jax
import jax.numpy as jnp
from jax import lax

D = 6144
DH = 128
LEN = 256
HEADS = 32
TOKENS = 8192
CAP = 16
N_MP = 16


def permute_rows(key, count, length):

    def one_perm(sub):
        return jax.random.permutation(sub, length)
    return jax.vmap(one_perm)(jax.random.split(key, count))


def draw_destination(key, part):
    n_seq = TOKENS // LEN
    others = n_seq - 1
    remaining = LEN - CAP
    base = remaining // others
    extra_count = remaining % others
    spread = min(base, CAP - base - 1)
    index = jnp.arange(others)
    jitter = jax.random.randint(jax.random.fold_in(key, 101), (others,), 0, spread + 1)
    signs = jnp.where(index % 2 == 0, 1, -1)
    lonely = jnp.logical_and(index == others - 1, others % 2 == 1)
    values = base + jnp.where(lonely, 0, signs * jitter[index // 2])
    order = jax.random.permutation(jax.random.fold_in(key, 102), others)
    values = values + (order < extra_count).astype(jnp.int32)
    cycle = jnp.concatenate([jnp.array([CAP], jnp.int32), values.astype(jnp.int32)])
    shift_by = jax.random.randint(jax.random.fold_in(key, 103), (), 0, n_seq)
    cycle = jnp.roll(cycle, shift_by)
    sigma = jax.random.permutation(jax.random.fold_in(key, 104), n_seq)
    sources = jnp.arange(n_seq)[:, None]
    counts = cycle[(sigma[None, :] - sources) % n_seq]
    inclusive = jnp.cumsum(counts, axis=1)
    row_start = inclusive - counts
    col_start = jnp.cumsum(counts, axis=0) - counts
    row_perm = permute_rows(jax.random.fold_in(key, 105), n_seq, LEN)
    place_perm = permute_rows(jax.random.fold_in(key, 106), n_seq, LEN)
    ranks = jnp.arange(LEN)
    owners = jnp.sum((inclusive[:, None, :] <= ranks[None, :, None]).astype(jnp.int32), axis=2)
    within = ranks[None, :] - jnp.take_along_axis(row_start, owners, axis=1)
    offset = jnp.take_along_axis(col_start, owners, axis=1) + within
    slot_rank = owners * LEN + place_perm[owners, offset]
    chosen = jnp.take_along_axis(slot_rank, row_perm, axis=1)
    return chosen.reshape(-1).astype(jnp.int32)


def draw_segment(key, part):
    n_seq = TOKENS // LEN
    biggest = min(64, LEN // 2)
    lengths = jax.random.randint(jax.random.fold_in(key, 201), (n_seq, LEN), 1, biggest + 1)
    chosen = jax.random.randint(jax.random.fold_in(key, 202), (n_seq,), 0, (LEN - biggest) // biggest + 1)
    slots = jnp.arange(LEN)
    lengths = jnp.where(slots[None, :] == chosen[:, None], biggest, lengths).astype(jnp.int32)
    starts = jnp.cumsum(lengths, axis=1) - lengths
    local = jnp.sum((starts[:, None, :] <= slots[None, :, None]).astype(jnp.int32), axis=2) - 1
    ids = local + jnp.arange(n_seq, dtype=jnp.int32)[:, None] * LEN
    return ids.reshape(-1).astype(jnp.int32)


def draw_patches(key, part):
    noise = jax.random.normal(jax.random.fold_in(key, 1), (TOKENS, D), jnp.float32)
    col_scale = jnp.exp(jax.random.uniform(jax.random.fold_in(key, 2), (D,), jnp.float32, math.log(0.3), math.log(3.0)))
    row_scale = jnp.exp(jax.random.uniform(jax.random.fold_in(key, 3), (TOKENS, 1), jnp.float32, math.log(0.3), math.log(3.0)))
    return (noise * col_scale[None, :] * row_scale).astype(jnp.bfloat16)


def draw_ln_gain(key, part):
    ramp = jnp.arange(D, dtype=jnp.float32) / (D - 1)
    factor = jnp.exp(jax.random.uniform(jax.random.fold_in(key, 11), (D,), jnp.float32, math.log(0.7), math.log(1.4)))
    return ((1.0 + 2.0 * ramp) * factor).astype(jnp.float32)


def projection(key, which):
    width = HEADS * DH
    scale = D ** (-0.5)
    shared = jax.random.normal(jax.random.fold_in(key, 21), (D, width), jnp.float32) * scale
    own = jax.random.normal(jax.random.fold_in(key, 22 + which), (D, width), jnp.float32) * scale
    matrix = shared if which == 0 else own
    return matrix.astype(jnp.bfloat16)


def draw_w_query(key, part):
    return projection(key, 0)


def draw_w_key(key, part):
    return projection(key, 1)


def draw_w_value(key, part):
    return projection(key, 2)


def head_gain(key, salt):
    low, high = (0.6, 1.8)
    per_head = jnp.exp(jax.random.uniform(jax.random.fold_in(key, salt), (HEADS, 1), jnp.float32, math.log(low), math.log(high)))
    per_channel = jax.random.uniform(jax.random.fold_in(key, salt + 1), (HEADS, DH), jnp.float32, 0.8, 1.25)
    return (per_head * per_channel).reshape(-1).astype(jnp.float32)


def draw_query_gain(key, part):
    return head_gain(key, 41)


def draw_key_gain(key, part):
    return head_gain(key, 51)


def block_scale(stream_key, dims, cuts, least, largest):
    loudness, own = 1.0, jax.random.fold_in(stream_key, 6)
    for dim, shards_of in cuts:
        draws = jnp.exp(jax.random.uniform(jax.random.fold_in(own, dim), (shards_of,), jnp.float32, least / len(cuts), largest / len(cuts)))
        loudness = loudness * jnp.repeat(draws, dims[dim] // shards_of).reshape([-1 if axis == dim else 1 for axis in range(len(dims))])
    return loudness


def normal_values(stream_key, shape, scale, most, pieces=(), kind=jnp.bfloat16):
    loudness = block_scale(stream_key, shape, pieces, -0.22, 0.18) if pieces else 1.0
    result = jax.random.normal(stream_key, shape, jnp.float32) * scale * loudness
    return jnp.minimum(jnp.maximum(result, -most), most).astype(kind)


def setup_inputs(seed: int = 0) -> dict:
    key_list = jax.random.split(jax.random.key(seed), 11)
    return {
        "patches": draw_patches(jax.random.fold_in(key_list[10], 71), 0),
        "destination": draw_destination(jax.random.fold_in(key_list[10], 71), 0),
        "segment": draw_segment(jax.random.fold_in(key_list[10], 71), 0),
        "ln_gain": draw_ln_gain(jax.random.fold_in(key_list[10], 71), 0),
        "w_query": draw_w_query(jax.random.fold_in(key_list[10], 71), 0),
        "w_key": draw_w_key(jax.random.fold_in(key_list[10], 71), 0),
        "w_value": draw_w_value(jax.random.fold_in(key_list[10], 71), 0),
        "query_gain": draw_query_gain(jax.random.fold_in(key_list[10], 71), 0),
        "key_gain": draw_key_gain(jax.random.fold_in(key_list[10], 71), 0),
        "attn_cotangent": normal_values(key_list[9], (TOKENS, HEADS * DH), 1.0, 6.0, ((0, 32), (1, 16))),
    }


EPSILON = 1e-06
NEGATIVE = -1e+30

def row_norm(values_in):
    row_mean = lax.optimization_barrier(jnp.mean(values_in, axis=-1, keepdims=True))
    centred = values_in - row_mean
    row_var = lax.optimization_barrier(jnp.mean(centred * centred, axis=-1, keepdims=True))
    inverse = lax.rsqrt(row_var + EPSILON)
    return (centred * inverse, inverse)

def norm_back(grad_hat, scaled, inverse):
    first = lax.optimization_barrier(jnp.mean(grad_hat, axis=-1, keepdims=True))
    second = lax.optimization_barrier(jnp.mean(grad_hat * scaled, axis=-1, keepdims=True))
    return (grad_hat - first - scaled * second) * inverse

def sequence_pass(packet):
    query_norm, key_norm, value_half, image_ids, cotangent = packet
    factor = 1.0 / math.sqrt(DH)
    scores = jnp.einsum('qhd,khd->hqk', query_norm.astype(jnp.float32), key_norm.astype(jnp.float32)) * factor
    same_image = image_ids[:, None] == image_ids[None, :]
    scores = jnp.where(same_image[None, :, :], scores, NEGATIVE)
    row_peak = lax.optimization_barrier(jnp.max(scores, axis=-1, keepdims=True))
    exp_scores = jnp.exp(scores - row_peak)
    prob_full = exp_scores / lax.optimization_barrier(jnp.sum(exp_scores, axis=-1, keepdims=True))
    prob_half = prob_full.astype(jnp.bfloat16)
    context = jnp.einsum('hqk,khd->qhd', prob_half.astype(jnp.float32), value_half.astype(jnp.float32)).astype(jnp.bfloat16)
    grad_prob = jnp.einsum('qhd,khd->hqk', cotangent.astype(jnp.float32), value_half.astype(jnp.float32))
    row_delta = lax.optimization_barrier(jnp.sum(prob_full * grad_prob, axis=-1, keepdims=True))
    grad_score = (prob_full * (grad_prob - row_delta) * factor).astype(jnp.bfloat16)
    query_side = jnp.einsum('hqk,khd->qhd', grad_score.astype(jnp.float32), key_norm.astype(jnp.float32))
    key_side = jnp.einsum('hqk,qhd->khd', grad_score.astype(jnp.float32), query_norm.astype(jnp.float32))
    value_grad = jnp.einsum('hqk,qhd->khd', prob_half.astype(jnp.float32), cotangent.astype(jnp.float32)).astype(jnp.bfloat16)
    return (context, query_side, key_side, value_grad)

def reference(patches, destination, segment, ln_gain, w_query, w_key, w_value, query_gain, key_gain, attn_cotangent):
    packed = jnp.zeros_like(patches).at[destination].set(patches)
    x_hat, inverse = row_norm(packed.astype(jnp.float32))
    normed = (x_hat * ln_gain).astype(jnp.bfloat16)
    query_raw = jnp.dot(normed, w_query, preferred_element_type=jnp.float32)
    key_raw = jnp.dot(normed, w_key, preferred_element_type=jnp.float32)
    value_raw = jnp.dot(normed, w_value, preferred_element_type=jnp.float32)
    tokens = packed.shape[0]
    heads = query_raw.shape[1] // DH
    query_hat, query_inv = row_norm(query_raw.reshape(tokens, heads, DH))
    key_hat, key_inv = row_norm(key_raw.reshape(tokens, heads, DH))
    qgain = query_gain.reshape(heads, DH)
    kgain = key_gain.reshape(heads, DH)
    query_norm = (query_hat * qgain).astype(jnp.bfloat16)
    key_norm = (key_hat * kgain).astype(jnp.bfloat16)
    value_half = value_raw.astype(jnp.bfloat16).reshape(tokens, heads, DH)
    groups = tokens // LEN
    shape_seq = (groups, LEN, heads, DH)
    context, query_side, key_side, value_grad = lax.map(sequence_pass, (query_norm.reshape(shape_seq), key_norm.reshape(shape_seq), value_half.reshape(shape_seq), segment.reshape(groups, LEN), attn_cotangent.reshape(shape_seq)))
    query_side = query_side.reshape(tokens, heads, DH)
    key_side = key_side.reshape(tokens, heads, DH)
    query_grad = norm_back(query_side * qgain, query_hat, query_inv).astype(jnp.bfloat16).reshape(tokens, heads * DH)
    key_grad = norm_back(key_side * kgain, key_hat, key_inv).astype(jnp.bfloat16).reshape(tokens, heads * DH)
    value_grad = value_grad.reshape(tokens, heads * DH)
    width = heads // N_MP * DH
    contract = (((1,), (1,)), ((), ()))

    def add_group(total, group):
        start = (group * width).astype(jnp.int32)
        term = lax.dot_general(lax.dynamic_slice_in_dim(query_grad, start, width, 1), lax.dynamic_slice_in_dim(w_query, start, width, 1), contract, preferred_element_type=jnp.float32)
        term = term + lax.dot_general(lax.dynamic_slice_in_dim(key_grad, start, width, 1), lax.dynamic_slice_in_dim(w_key, start, width, 1), contract, preferred_element_type=jnp.float32)
        term = term + lax.dot_general(lax.dynamic_slice_in_dim(value_grad, start, width, 1), lax.dynamic_slice_in_dim(w_value, start, width, 1), contract, preferred_element_type=jnp.float32)
        rounded = lax.optimization_barrier(term.astype(jnp.bfloat16)).astype(jnp.float32)
        return (total + rounded, None)
    grad_normed, unused = lax.scan(add_group, jnp.zeros((tokens, packed.shape[1]), jnp.float32), jnp.arange(N_MP, dtype=jnp.int32))
    grad_packed = norm_back(grad_normed * ln_gain, x_hat, inverse).astype(jnp.bfloat16)
    return (context.reshape(tokens, heads * DH), grad_packed)
```

```python
import functools
import math

import jax
import jax.numpy as jnp
from jax import lax
from jax.experimental import pallas as pl
from jax.experimental.pallas import tpu as pltpu
from jax.sharding import Mesh, PartitionSpec as P

D = 6144
DH = 128
LEN = 256
CAP = 16
NZ, NX, NY, NH, NC = 8, 4, 4, 2, 2
SHARD = D // (NY * NH * NC)
BLOCK = D // (NZ * NX)
EPSILON = 1e-06
NEGATIVE = -1e30
BF = jnp.bfloat16
F32 = jnp.float32
FOLD = [0, 2, 4, 6, 7, 5, 3, 1]
Z_RING = [(FOLD[i], FOLD[(i + 1) % NZ]) for i in range(NZ)]
Z_BACK = [(b, a) for a, b in Z_RING]
EARLY = (0, 1, -1, 2, -2)
LATE = (3, -3, 4)
TAIL = 16


def shift(n, k):
    return [(i, (i + k) % n) for i in range(n)]


def core_ring(n):
    return [(i * NC + k, (i + (1, n - 1)[k]) % n * NC + k) for i in range(n) for k in range(NC)]


def after(value, other):
    return value + other[(0,) * other.ndim] * 0


def contract(a, b, dim_a, dim_b):
    return lax.dot_general(
        a, b, (((dim_a,), (dim_b,)), ((), ())), preferred_element_type=F32
    )


def ring_source(place, core, steps, n):
    return lax.rem(place + jnp.where(core == 0, n - steps, steps), n)


def norm_kernel(where_ref, gain_ref, *rest):
    y, zh, c = where_ref[0], where_ref[1], where_ref[2]
    own, others = rest[:NY], rest[NY:NY + 2]
    normed_ref, packed_ref, stat_ref = rest[NY + 2:]
    blocks = []
    for steps in range(NY):
        for flip in range(NH):
            half = lax.rem(zh + flip, NH)
            there = ring_source(y, c, steps, NY) * NH + half
            blocks.append((own[steps], flip, there * NC + c))
            there = ring_source(y, 1 - c, steps, NY) * NH + half
            ref, i = (others[0], 2 * steps + flip) if steps < NY - 1 else (others[1], flip)
            blocks.append((ref, i, there * NC + (1 - c)))
    total = jnp.zeros((1, LEN), F32)
    for ref, i, _ in blocks:
        total = total + jnp.sum(ref[i].astype(F32), axis=0, keepdims=True)
    mean = total / D
    total = jnp.zeros((1, LEN), F32)
    for ref, i, _ in blocks:
        centred = ref[i].astype(F32) - mean
        total = total + jnp.sum(centred * centred, axis=0, keepdims=True)
    inverse = lax.rsqrt(total / D + EPSILON)
    stat_ref[0:1, :] = mean
    stat_ref[1:2, :] = inverse
    for ref, i, index in blocks:
        rows = pl.ds(pl.multiple_of(index * SHARD, SHARD), SHARD)
        value = ref[i]
        packed_ref[rows, :] = value
        normed_ref[rows, :] = (
            (value.astype(F32) - mean) * inverse * gain_ref[rows, :]
        ).astype(BF)


def row_norm(values_in):
    row_mean = jnp.mean(values_in, axis=-1, keepdims=True)
    centred = values_in - row_mean
    row_var = jnp.mean(centred * centred, axis=-1, keepdims=True)
    inverse = lax.rsqrt(row_var + EPSILON)
    return centred * inverse, inverse


def norm_back(grad_hat, scaled, inverse):
    first = jnp.mean(grad_hat, axis=-1, keepdims=True)
    second = jnp.mean(grad_hat * scaled, axis=-1, keepdims=True)
    return (grad_hat - first - scaled * second) * inverse


def weight_blocks(where_ref):
    c, zl, x = where_ref[2], where_ref[3], where_ref[4]
    position = jnp.where(lax.rem(zl, 2) == 0, zl // 2, 7 - zl // 2)
    found = []
    for early, steps in ((True, EARLY), (False, LATE)):
        for off in range(NX):
            x_from = off if early else ring_source(x, c, off, NX)
            for j, step in enumerate(steps):
                p = lax.rem(position - step + NZ, NZ)
                z_from = jnp.where(p < 4, 2 * p, 15 - 2 * p)
                found.append((early, off, j, z_from * NX + x_from))
    return found


def block_rows(block):
    return pl.ds(pl.multiple_of(block * BLOCK, BLOCK), BLOCK)


def first_kernel(where_ref, normed_ref, early_ref, late0_ref, late1_ref, late2_ref,
                 acc_ref, weight_ref, sems):
    late_refs = (late0_ref, late1_ref, late2_ref)
    blocks = weight_blocks(where_ref)
    count = NX * len(EARLY) + (NX - 1) * len(LATE)
    copies = []
    for n in range(2 * NX - 1):
        slot = n * len(EARLY) if n < NX else NX * len(EARLY) + (n - NX) * len(LATE)
        size = len(EARLY) if n < NX else len(LATE)
        source = early_ref.at[n] if n < NX else late_refs[n - NX]
        copy = pltpu.make_async_copy(source, weight_ref.at[slot:slot + size], sems.at[n])
        copy.start()
        copies.append((slot, copy))
    copies = dict(copies)
    for slot in range(count):
        if slot in copies:
            copies[slot].wait()
        part = contract(normed_ref[block_rows(blocks[slot][3]), :], weight_ref[slot], 0, 0)
        if slot == 0:
            acc_ref[...] = part
        else:
            acc_ref[...] += part


def main_kernel(where_ref, gain_ref, stat_ref, seg_row_ref, seg_col_ref, qgain_ref, kgain_ref,
                cot_ref, part_ref, normed_ref, packed_hbm, early_ref, *rest):
    late_refs, rest = rest[:NX], rest[NX:]
    attn_ref, keep_a, keep_b, give_a, give_b = rest[:5]
    weight_ref, rows_ref, packed_ref, acc_ref, grad_ref, sems = rest[5:]
    y, zh, c = where_ref[0], where_ref[1], where_ref[2]
    blocks = weight_blocks(where_ref)
    first_late = NX * len(EARLY)
    final = first_late + (NX - 1) * len(LATE)

    arrived = []
    order = [2 * NX - 1] + list(range(2 * NX - 1))
    for n in order:
        slot = n * len(EARLY) if n < NX else first_late + (n - NX) * len(LATE)
        size = len(EARLY) if n < NX else len(LATE)
        source = early_ref.at[n] if n < NX else late_refs[n - NX]
        copy = pltpu.make_async_copy(source, weight_ref.at[slot:slot + size], sems.at[n])
        copy.start()
        arrived.append((slot, copy))
        if n == 2 * NX - 1:
            for j in range(len(LATE)):
                copy = pltpu.make_async_copy(
                    normed_ref.at[block_rows(blocks[final + j][3]), :],
                    rows_ref.at[j], sems.at[2 * NX + j])
                copy.start()
                arrived.append((-1 - j, copy))
    arrived = dict(arrived)
    packed_copy = pltpu.make_async_copy(packed_hbm, packed_ref, sems.at[2 * NX + len(LATE)])
    packed_copy.start()

    arrived.pop(final).wait()
    for j in range(len(LATE)):
        arrived.pop(-1 - j).wait()
        part = contract(rows_ref[j], weight_ref[final + j], 0, 0)
        if j == 0:
            acc_ref[...] = part_ref[...] + part
        else:
            acc_ref[...] += part

    factor = 1.0 / math.sqrt(DH)
    same = seg_col_ref[...] == seg_row_ref[...]
    width = qgain_ref.shape[1]
    for h in range(width // DH):
        cols = slice(h * DH, (h + 1) * DH)
        qgain, kgain = qgain_ref[:, cols], kgain_ref[:, cols]
        query_hat, query_inv = row_norm(acc_ref[:, h * DH:(h + 1) * DH])
        key_hat, key_inv = row_norm(acc_ref[:, width + h * DH:width + (h + 1) * DH])
        value = acc_ref[:, 2 * width + h * DH:2 * width + (h + 1) * DH].astype(BF)
        query = (query_hat * qgain).astype(BF)
        key = (key_hat * kgain).astype(BF)
        cot = cot_ref[:, cols]
        scores = jnp.where(same, contract(query, key, 1, 1) * factor, NEGATIVE)
        exp_scores = jnp.exp(scores - jnp.max(scores, axis=-1, keepdims=True))
        prob = exp_scores / jnp.sum(exp_scores, axis=-1, keepdims=True)
        prob_half = prob.astype(BF)
        attn_ref[:, cols] = contract(prob_half, value, 1, 0).astype(BF)
        grad_prob = contract(cot, value, 1, 1)
        delta = jnp.sum(prob * grad_prob, axis=-1, keepdims=True)
        grad_score = (prob * (grad_prob - delta) * factor).astype(BF)
        query_side = contract(grad_score, key, 1, 0)
        key_side = contract(grad_score, query, 0, 0)
        grad_ref[:, h * DH:(h + 1) * DH] = norm_back(
            query_side * qgain, query_hat, query_inv).astype(BF)
        grad_ref[:, width + h * DH:width + (h + 1) * DH] = norm_back(
            key_side * kgain, key_hat, key_inv).astype(BF)
        grad_ref[:, 2 * width + h * DH:2 * width + (h + 1) * DH] = contract(
            prob_half, cot, 0, 0).astype(BF)

    mean, inverse = stat_ref[0:1, :], stat_ref[1:2, :]
    first = jnp.zeros((1, LEN), F32)
    second = jnp.zeros((1, LEN), F32)
    packed_copy.wait()
    for slot, (_, _, _, block) in enumerate(blocks):
        if slot in arrived:
            arrived[slot].wait()
        rows = block_rows(block)
        term = contract(weight_ref[slot], grad_ref[...], 1, 1).astype(BF)
        scaled = term.astype(F32) * gain_ref[rows, :]
        first = first + jnp.sum(scaled, axis=0, keepdims=True)
        second = second + jnp.sum(
            scaled * (packed_ref[rows, :].astype(F32) - mean), axis=0, keepdims=True)
        same_core = lax.rem(block // 2, NC) == c
        same_half = lax.rem(block // 4, NH) == zh
        target = (block // 8) * SHARD + lax.rem(block, 2) * BLOCK
        out = pl.ds(pl.multiple_of(target, BLOCK), BLOCK)
        for core_flag, half_flag, ref in (
            (True, True, keep_a), (True, False, keep_b),
            (False, True, give_a), (False, False, give_b),
        ):
            @pl.when(jnp.logical_and(same_core == core_flag, same_half == half_flag))
            def _(ref=ref):
                ref[out, :] = term

    sums = split_sums(first, second * inverse)
    keep_b[NY * SHARD:, :] = sums
    give_b[NY * SHARD:, :] = sums


def split_sums(first, second):
    rows = []
    for value in (first, second):
        for _ in range(3):
            piece = value.astype(BF)
            rows.append(piece.astype(F32))
            value = value - piece.astype(F32)
    rows.append(jnp.zeros((TAIL - len(rows), LEN), F32))
    return jnp.concatenate(rows, axis=0).astype(BF)


def join_sums(tail):
    tail = tail.astype(F32)
    return (
        tail[..., 0:1, :] + tail[..., 1:2, :] + tail[..., 2:3, :],
        tail[..., 3:4, :] + tail[..., 4:5, :] + tail[..., 5:6, :],
    )


def send_packets(patches, destination):
    rows = patches.shape[0]
    n_groups = NZ * NX
    owners = destination // LEN
    offsets = destination % LEN
    one_hot = (owners[:, None] == jnp.arange(n_groups)[None, :]).astype(BF)
    index = jnp.arange(rows)
    strict = (index[:, None] > index[None, :]).astype(BF)
    earlier = jnp.dot(strict, one_hot, preferred_element_type=F32)
    rank = jnp.sum(earlier * one_hot.astype(F32), axis=1).astype(jnp.int32)
    position = owners * CAP + rank
    placing = jnp.arange(n_groups * CAP)[:, None] == position[None, :]
    sent = jnp.dot(placing.astype(BF), patches, preferred_element_type=F32).astype(BF)
    places = jnp.sum(jnp.where(placing, offsets[None, :] + 1, 0), axis=1)
    places = places.reshape(n_groups, 1, CAP).astype(BF)
    places = jnp.pad(places, ((0, 0), (0, 7), (0, 128 - CAP)))
    blocks = [
        sent[:, i:i + 128].reshape(n_groups, CAP, 128) for i in range(0, sent.shape[1], 128)
    ]
    return jnp.concatenate(blocks + [places], axis=1)


def unpack(got):
    n_groups = got.shape[0]
    n_blocks = (got.shape[1] - 8) // CAP
    places = got[:, n_blocks * CAP, :CAP].astype(jnp.int32).reshape(n_groups * CAP) - 1
    chosen = (places[:, None] == jnp.arange(LEN)[None, :]).astype(BF)
    out = [
        contract(
            got[:, i * CAP:(i + 1) * CAP].reshape(n_groups * CAP, 128), chosen, 0, 0
        ).astype(BF)
        for i in range(n_blocks)
    ]
    return jnp.concatenate(out, axis=0)


def per_device(patches, destination, segment, ln_gain, w_query, w_key, w_value,
               query_gain, key_gain, attn_cotangent):
    y, zh, c = lax.axis_index("y"), lax.axis_index("zh"), lax.axis_index("c")
    zl, x = lax.axis_index("zl"), lax.axis_index("x")
    where = jnp.stack([y, zh, c, zl, x]).astype(jnp.int32)
    gain_column = ln_gain[:, None]

    weight = jnp.concatenate([w_query, w_key, w_value], axis=1)
    packets = send_packets(patches, destination)

    x_ring = functools.partial(lax.ppermute, axis_name=("x", "c"), perm=core_ring(NX))
    y_ring = functools.partial(lax.ppermute, axis_name=("y", "c"), perm=core_ring(NY))
    got = lax.all_to_all(packets, ("zl", "x"), split_axis=0, concat_axis=0, tiled=True)
    z = {0: weight}
    for step in (1, 2, 3, 4):
        block = z[step - 1]
        z[step] = lax.ppermute(after(block, got) if step == 2 else block, "zl", Z_RING)
        if step < 4:
            z[-step] = lax.ppermute(z[1 - step], "zl", Z_BACK)
    early = lax.all_gather(jnp.concatenate([z[n] for n in EARLY]), "x", axis=0, tiled=True)
    early = early.reshape((NX, len(EARLY)) + weight.shape)
    late = [jnp.stack([z[n] for n in LATE])]
    for _ in range(NX - 1):
        late.append(x_ring(late[-1]))

    mine = unpack(got)
    g = [jnp.stack([mine, lax.ppermute(mine, "zh", shift(NH, 1))])]
    for _ in range(NY - 1):
        g.append(y_ring(g[-1]))
    most = lax.ppermute(jnp.concatenate(g[:3]), "c", shift(NC, 1))
    last = lax.ppermute(g[3], "c", shift(NC, 1))

    vmem = pl.BlockSpec(memory_space=pltpu.VMEM)
    smem = pl.BlockSpec(memory_space=pltpu.SMEM)
    normed, packed, stat = pl.pallas_call(
        norm_kernel,
        out_shape=(
            jax.ShapeDtypeStruct((D, LEN), BF),
            jax.ShapeDtypeStruct((D, LEN), BF),
            jax.ShapeDtypeStruct((2, LEN), F32),
        ),
        in_specs=[smem] + [vmem] * 7,
        out_specs=(vmem, vmem, vmem),
        compiler_params=pltpu.CompilerParams(vmem_limit_bytes=32 << 20),
        cost_estimate=pl.CostEstimate(flops=20_000_000, bytes_accessed=10_000_000, transcendentals=0),
        name="norm",
    )(where, gain_column, *g, most, last)

    width = w_query.shape[1]
    hbm = pl.BlockSpec(memory_space=pl.ANY)
    n_first = NX * len(EARLY) + (NX - 1) * len(LATE)
    part = pl.pallas_call(
        first_kernel,
        out_shape=jax.ShapeDtypeStruct((LEN, 3 * width), F32),
        in_specs=[smem, vmem] + [hbm] * NX,
        out_specs=vmem,
        scratch_shapes=[
            pltpu.VMEM((n_first,) + weight.shape, BF),
            pltpu.SemaphoreType.DMA((2 * NX - 1,)),
        ],
        compiler_params=pltpu.CompilerParams(vmem_limit_bytes=24 << 20),
        cost_estimate=pl.CostEstimate(
            flops=2_200_000_000, bytes_accessed=12_000_000, transcendentals=0),
        name="first",
    )(where, normed, early, *late[:NX - 1])

    half = jax.ShapeDtypeStruct((NY * SHARD, LEN), BF)
    half_tail = jax.ShapeDtypeStruct((NY * SHARD + TAIL, LEN), BF)
    context, keep_a, keep_b, give_a, give_b = pl.pallas_call(
        main_kernel,
        out_shape=(jax.ShapeDtypeStruct((LEN, width), BF), half, half_tail, half, half_tail),
        in_specs=[smem] + [vmem] * 8 + [hbm] * (3 + NX),
        out_specs=(vmem,) * 5,
        scratch_shapes=[
            pltpu.VMEM((NZ * NX,) + weight.shape, BF),
            pltpu.VMEM((len(LATE), BLOCK, LEN), BF),
            pltpu.VMEM((D, LEN), BF),
            pltpu.VMEM((LEN, 3 * width), F32),
            pltpu.VMEM((LEN, 3 * width), BF),
            pltpu.SemaphoreType.DMA((2 * NX + len(LATE) + 1,)),
        ],
        compiler_params=pltpu.CompilerParams(vmem_limit_bytes=36 << 20),
        cost_estimate=pl.CostEstimate(
            flops=3_000_000_000, bytes_accessed=20_000_000, transcendentals=131072),
        name="core",
    )(where, gain_column, stat, segment[None, :], segment[:, None], query_gain[None, :],
      key_gain[None, :], attn_cotangent, part, normed, packed, early, *late)

    rows = NY * SHARD
    y_swap = functools.partial(
        lax.all_to_all, axis_name="y", split_axis=0, concat_axis=0, tiled=True)
    taken = lax.ppermute(give_b, "c", shift(NC, 1))
    tails = [a + b for a, b in zip(join_sums(keep_b[rows:]), join_sums(taken[rows:]))]
    both = (keep_b[:rows].astype(F32) + taken[:rows].astype(F32)).astype(BF)
    tail = jnp.broadcast_to(split_sums(*tails)[None], (NY, TAIL, LEN))
    got_b = y_swap(jnp.concatenate([both.reshape(NY, SHARD, LEN), tail], axis=1))
    taken = lax.ppermute(give_a, "c", shift(NC, 1))
    both = (keep_a.astype(F32) + taken.astype(F32)).astype(BF)
    got_a = y_swap(both.reshape(NY, SHARD, LEN))
    leave = jnp.sum(got_b[:, :SHARD].astype(F32), axis=0).astype(BF)
    sums = [jnp.sum(a, axis=0) for a in join_sums(got_b[:, SHARD:])]
    came = lax.ppermute(
        jnp.concatenate([leave, split_sums(*sums)], axis=0), "zh", shift(NH, 1))
    shard = jnp.sum(got_a.astype(F32), axis=0) + came[:SHARD].astype(F32)
    first, second = [a + b for a, b in zip(sums, join_sums(came[SHARD:]))]

    index = (y * NH + zh) * NC + c
    gain_here = lax.dynamic_slice_in_dim(ln_gain, index * SHARD, SHARD, 0)[:, None]
    mean, inverse = stat[0:1], stat[1:2]
    x_hat = (mine.astype(F32) - mean) * inverse
    grad = (shard * gain_here - first / D - x_hat * (second / D)) * inverse
    return context, grad.T.astype(BF)


def solution(mesh):
    fine = Mesh(mesh.devices.reshape(NZ, NX, NY, NH, NC), ("zl", "x", "y", "zh", "c"))
    dp, mp = ("zl", "x"), ("y", "zh", "c")
    placed = (
        P(dp, mp), P(dp), P(dp), P(), P(dp, mp), P(dp, mp), P(dp, mp), P(mp), P(mp), P(dp, mp),
    )
    return jax.shard_map(
        per_device,
        mesh=fine,
        in_specs=placed,
        out_specs=(P(dp, mp), P(dp, mp)),
        check_vma=False,
    )
```

```python
import functools
import math

import jax
import jax.numpy as jnp
from jax import lax
from jax.experimental import pallas as pl
from jax.experimental.pallas import tpu as pltpu
from jax.sharding import Mesh, PartitionSpec as P

D = 6144
DH = 128
LEN = 256
CAP = 16
NZ, NX, NY, NH, NC = 8, 4, 4, 2, 2
SHARD = D // (NY * NH * NC)
BLOCK = D // (NZ * NX)
EPSILON = 1e-06
NEGATIVE = -1e30
BF = jnp.bfloat16
F32 = jnp.float32
FOLD = [0, 2, 4, 6, 7, 5, 3, 1]
Z_RING = [(FOLD[i], FOLD[(i + 1) % NZ]) for i in range(NZ)]
Z_BACK = [(b, a) for a, b in Z_RING]
Z_TWO = [(FOLD[i], FOLD[(i + 2) % NZ]) for i in range(NZ)]
EARLY = (0, 1, -1, 2, -2)
FIRST = 1
LATE = (3, -3, 4)
TAIL = 16


def shift(n, k):
    return [(i, (i + k) % n) for i in range(n)]


def core_ring(n):
    return [(i * NC + k, (i + (1, n - 1)[k]) % n * NC + k) for i in range(n) for k in range(NC)]


def after(value, other):
    return value + other[(0,) * other.ndim] * 0


def contract(a, b, dim_a, dim_b):
    return lax.dot_general(
        a, b, (((dim_a,), (dim_b,)), ((), ())), preferred_element_type=F32
    )


def ring_source(place, core, steps, n):
    return lax.rem(place + jnp.where(core == 0, n - steps, steps), n)


def norm_kernel(where_ref, gain_ref, *rest):
    y, zh, c = where_ref[0], where_ref[1], where_ref[2]
    own, others = rest[:NY], rest[NY:NY + 2]
    normed_ref, packed_ref, stat_ref = rest[NY + 2:]
    blocks = []
    for steps in range(NY):
        for flip in range(NH):
            half = lax.rem(zh + flip, NH)
            there = ring_source(y, c, steps, NY) * NH + half
            blocks.append((own[steps], flip, there * NC + c))
            there = ring_source(y, 1 - c, steps, NY) * NH + half
            ref, i = (others[0], 2 * steps + flip) if steps < NY - 1 else (others[1], flip)
            blocks.append((ref, i, there * NC + (1 - c)))
    total = jnp.zeros((1, LEN), F32)
    for ref, i, _ in blocks:
        total = total + jnp.sum(ref[i].astype(F32), axis=0, keepdims=True)
    mean = total / D
    total = jnp.zeros((1, LEN), F32)
    for ref, i, _ in blocks:
        centred = ref[i].astype(F32) - mean
        total = total + jnp.sum(centred * centred, axis=0, keepdims=True)
    inverse = lax.rsqrt(total / D + EPSILON)
    stat_ref[0:1, :] = mean
    stat_ref[1:2, :] = inverse
    for ref, i, index in blocks:
        rows = pl.ds(pl.multiple_of(index * SHARD, SHARD), SHARD)
        value = ref[i]
        packed_ref[rows, :] = value
        normed_ref[rows, :] = (
            (value.astype(F32) - mean) * inverse * gain_ref[rows, :]
        ).astype(BF)


def row_norm(values_in):
    row_mean = jnp.mean(values_in, axis=-1, keepdims=True)
    centred = values_in - row_mean
    row_var = jnp.mean(centred * centred, axis=-1, keepdims=True)
    inverse = lax.rsqrt(row_var + EPSILON)
    return centred * inverse, inverse


def norm_back(grad_hat, scaled, inverse):
    first = jnp.mean(grad_hat, axis=-1, keepdims=True)
    second = jnp.mean(grad_hat * scaled, axis=-1, keepdims=True)
    return (grad_hat - first - scaled * second) * inverse


def weight_blocks(where_ref):
    c, zl, x = where_ref[2], where_ref[3], where_ref[4]
    position = jnp.where(lax.rem(zl, 2) == 0, zl // 2, 7 - zl // 2)
    found = []
    for steps in (EARLY[:FIRST], EARLY[FIRST:], LATE):
        for off in range(NX):
            x_from = ring_source(x, c, off, NX) if steps is LATE else off
            for step in steps:
                p = lax.rem(position - step + NZ, NZ)
                z_from = jnp.where(p < 4, 2 * p, 15 - 2 * p)
                found.append(z_from * NX + x_from)
    return found


def block_rows(block):
    return pl.ds(pl.multiple_of(block * BLOCK, BLOCK), BLOCK)


def load_weights(early_refs, late_refs, weight_ref, sems):
    sources = []
    for ref in early_refs:
        sources.extend((ref.at[off], ref.shape[1]) for off in range(NX))
    sources.extend((ref, ref.shape[0]) for ref in late_refs)
    copies = {}
    slot = 0
    for n, (source, size) in enumerate(sources):
        copies[slot] = pltpu.make_async_copy(
            source, weight_ref.at[slot:slot + size], sems.at[n])
        slot += size
    return copies


def first_kernel(where_ref, normed_ref, early0_ref, early1_ref, late0_ref, late1_ref, late2_ref,
                 acc_ref, weight_ref, sems):
    blocks = weight_blocks(where_ref)
    copies = load_weights(
        (early0_ref, early1_ref), (late0_ref, late1_ref, late2_ref), weight_ref, sems)
    for copy in copies.values():
        copy.start()
    for slot in range(weight_ref.shape[0]):
        if slot in copies:
            copies[slot].wait()
        part = contract(normed_ref[block_rows(blocks[slot]), :], weight_ref[slot], 0, 0)
        if slot == 0:
            acc_ref[...] = part
        else:
            acc_ref[...] += part


def main_kernel(where_ref, gain_ref, stat_ref, seg_row_ref, seg_col_ref, qgain_ref, kgain_ref,
                cot_ref, part_ref, normed_ref, packed_hbm, *rest):
    early_refs, late_refs, rest = rest[:2], rest[2:2 + NX], rest[2 + NX:]
    attn_ref, keep_a, keep_b, give_a, give_b = rest[:5]
    weight_ref, rows_ref, packed_ref, acc_ref, grad_ref, sems = rest[5:]
    zh, c = where_ref[1], where_ref[2]
    blocks = weight_blocks(where_ref)
    final = NZ * NX - len(LATE)

    arrived = load_weights(early_refs, late_refs, weight_ref, sems)
    last_copy = arrived.pop(final)
    last_copy.start()
    row_copies = [
        pltpu.make_async_copy(
            normed_ref.at[block_rows(blocks[final + j]), :], rows_ref.at[j], sems.at[3 * NX + j])
        for j in range(len(LATE))
    ]
    packed_copy = pltpu.make_async_copy(packed_hbm, packed_ref, sems.at[3 * NX + len(LATE)])
    for copy in row_copies + list(arrived.values()) + [packed_copy]:
        copy.start()

    last_copy.wait()
    for j, copy in enumerate(row_copies):
        copy.wait()
        part = contract(rows_ref[j], weight_ref[final + j], 0, 0)
        if j == 0:
            acc_ref[...] = part_ref[...] + part
        else:
            acc_ref[...] += part

    factor = 1.0 / math.sqrt(DH)
    same = seg_col_ref[...] == seg_row_ref[...]
    width = qgain_ref.shape[1]
    for h in range(width // DH):
        cols = slice(h * DH, (h + 1) * DH)
        qgain, kgain = qgain_ref[:, cols], kgain_ref[:, cols]
        query_hat, query_inv = row_norm(acc_ref[:, h * DH:(h + 1) * DH])
        key_hat, key_inv = row_norm(acc_ref[:, width + h * DH:width + (h + 1) * DH])
        value = acc_ref[:, 2 * width + h * DH:2 * width + (h + 1) * DH].astype(BF)
        query = (query_hat * qgain).astype(BF)
        key = (key_hat * kgain).astype(BF)
        cot = cot_ref[:, cols]
        scores = jnp.where(same, contract(query, key, 1, 1) * factor, NEGATIVE)
        exp_scores = jnp.exp(scores - jnp.max(scores, axis=-1, keepdims=True))
        prob = exp_scores / jnp.sum(exp_scores, axis=-1, keepdims=True)
        prob_half = prob.astype(BF)
        attn_ref[:, cols] = contract(prob_half, value, 1, 0).astype(BF)
        grad_prob = contract(cot, value, 1, 1)
        delta = jnp.sum(prob * grad_prob, axis=-1, keepdims=True)
        grad_score = (prob * (grad_prob - delta) * factor).astype(BF)
        query_side = contract(grad_score, key, 1, 0)
        key_side = contract(grad_score, query, 0, 0)
        grad_ref[:, h * DH:(h + 1) * DH] = norm_back(
            query_side * qgain, query_hat, query_inv).astype(BF)
        grad_ref[:, width + h * DH:width + (h + 1) * DH] = norm_back(
            key_side * kgain, key_hat, key_inv).astype(BF)
        grad_ref[:, 2 * width + h * DH:2 * width + (h + 1) * DH] = contract(
            prob_half, cot, 0, 0).astype(BF)

    mean, inverse = stat_ref[0:1, :], stat_ref[1:2, :]
    first = jnp.zeros((1, LEN), F32)
    second = jnp.zeros((1, LEN), F32)
    packed_copy.wait()
    for slot, block in enumerate(blocks):
        if slot in arrived:
            arrived[slot].wait()
        rows = block_rows(block)
        term = contract(weight_ref[slot], grad_ref[...], 1, 1).astype(BF)
        scaled = term.astype(F32) * gain_ref[rows, :]
        first = first + jnp.sum(scaled, axis=0, keepdims=True)
        second = second + jnp.sum(
            scaled * (packed_ref[rows, :].astype(F32) - mean), axis=0, keepdims=True)
        same_core = lax.rem(block // 2, NC) == c
        same_half = lax.rem(block // 4, NH) == zh
        target = (block // 8) * SHARD + lax.rem(block, 2) * BLOCK
        out = pl.ds(pl.multiple_of(target, BLOCK), BLOCK)
        for core_flag, half_flag, ref in (
            (True, True, keep_a), (True, False, keep_b),
            (False, True, give_a), (False, False, give_b),
        ):
            @pl.when(jnp.logical_and(same_core == core_flag, same_half == half_flag))
            def _(ref=ref):
                ref[out, :] = term

    sums = split_sums(first, second * inverse)
    keep_b[NY * SHARD:, :] = sums
    give_b[NY * SHARD:, :] = sums


def split_sums(first, second):
    rows = []
    for value in (first, second):
        for _ in range(3):
            piece = value.astype(BF)
            rows.append(piece.astype(F32))
            value = value - piece.astype(F32)
    rows.append(jnp.zeros((TAIL - len(rows), LEN), F32))
    return jnp.concatenate(rows, axis=0).astype(BF)


def join_sums(tail):
    tail = tail.astype(F32)
    return (
        tail[..., 0:1, :] + tail[..., 1:2, :] + tail[..., 2:3, :],
        tail[..., 3:4, :] + tail[..., 4:5, :] + tail[..., 5:6, :],
    )


def send_packets(patches, destination):
    rows = patches.shape[0]
    n_groups = NZ * NX
    owners = destination // LEN
    offsets = destination % LEN
    one_hot = (owners[:, None] == jnp.arange(n_groups)[None, :]).astype(BF)
    index = jnp.arange(rows)
    strict = (index[:, None] > index[None, :]).astype(BF)
    earlier = jnp.dot(strict, one_hot, preferred_element_type=F32)
    rank = jnp.sum(earlier * one_hot.astype(F32), axis=1).astype(jnp.int32)
    position = owners * CAP + rank
    placing = jnp.arange(n_groups * CAP)[:, None] == position[None, :]
    sent = jnp.dot(placing.astype(BF), patches, preferred_element_type=F32).astype(BF)
    places = jnp.sum(jnp.where(placing, offsets[None, :] + 1, 0), axis=1)
    places = places.reshape(n_groups, 1, CAP).astype(BF)
    places = jnp.pad(places, ((0, 0), (0, 7), (0, 128 - CAP)))
    blocks = [
        sent[:, i:i + 128].reshape(n_groups, CAP, 128) for i in range(0, sent.shape[1], 128)
    ]
    return jnp.concatenate(blocks + [places], axis=1)


def unpack(got):
    n_groups = got.shape[0]
    n_blocks = (got.shape[1] - 8) // CAP
    places = got[:, n_blocks * CAP, :CAP].astype(jnp.int32).reshape(n_groups * CAP) - 1
    chosen = (places[:, None] == jnp.arange(LEN)[None, :]).astype(BF)
    out = [
        contract(
            got[:, i * CAP:(i + 1) * CAP].reshape(n_groups * CAP, 128), chosen, 0, 0
        ).astype(BF)
        for i in range(n_blocks)
    ]
    return jnp.concatenate(out, axis=0)


def per_device(patches, destination, segment, ln_gain, w_query, w_key, w_value,
               query_gain, key_gain, attn_cotangent):
    y, zh, c = lax.axis_index("y"), lax.axis_index("zh"), lax.axis_index("c")
    zl, x = lax.axis_index("zl"), lax.axis_index("x")
    where = jnp.stack([y, zh, c, zl, x]).astype(jnp.int32)
    gain_column = ln_gain[:, None]

    weight = jnp.concatenate([w_query, w_key, w_value], axis=1)
    packets = send_packets(patches, destination)

    x_ring = functools.partial(lax.ppermute, axis_name=("x", "c"), perm=core_ring(NX))
    y_ring = functools.partial(lax.ppermute, axis_name=("y", "c"), perm=core_ring(NY))
    got = lax.all_to_all(packets, ("zl", "x"), split_axis=0, concat_axis=0, tiled=True)
    mine = unpack(got)
    partner = lax.ppermute(mine, "zh", shift(NH, 1))
    z = {0: weight}
    z[1] = lax.ppermute(weight, "zl", Z_RING)
    z[-1] = lax.ppermute(weight, "zl", Z_BACK)
    z[2] = lax.ppermute(weight, "zl", Z_TWO)
    z[-2] = lax.ppermute(weight, "zl", [(b, a) for a, b in Z_TWO])
    z[3] = lax.ppermute(after(z[2], got), "zl", Z_RING)
    z[-3] = lax.ppermute(z[-2], "zl", Z_BACK)
    z[4] = lax.ppermute(after(z[3], partner), "zl", Z_RING)
    early = []
    for steps in (EARLY[:FIRST], EARLY[FIRST:]):
        joined = lax.all_gather(
            jnp.concatenate([after(z[n], got) if n == 1 else z[n] for n in steps]),
            "x", axis=0, tiled=True)
        early.append(joined.reshape((NX, len(steps)) + weight.shape))
    late = [jnp.stack([z[n] for n in LATE])]
    for _ in range(NX - 1):
        late.append(x_ring(late[-1]))

    g = [jnp.stack([mine, partner])]
    for _ in range(NY - 1):
        g.append(y_ring(g[-1]))
    most = lax.ppermute(jnp.concatenate(g[:3]), "c", shift(NC, 1))
    last = lax.ppermute(g[3], "c", shift(NC, 1))

    vmem = pl.BlockSpec(memory_space=pltpu.VMEM)
    smem = pl.BlockSpec(memory_space=pltpu.SMEM)
    normed, packed, stat = pl.pallas_call(
        norm_kernel,
        out_shape=(
            jax.ShapeDtypeStruct((D, LEN), BF),
            jax.ShapeDtypeStruct((D, LEN), BF),
            jax.ShapeDtypeStruct((2, LEN), F32),
        ),
        in_specs=[smem] + [vmem] * 7,
        out_specs=(vmem, vmem, vmem),
        compiler_params=pltpu.CompilerParams(vmem_limit_bytes=32 << 20),
        cost_estimate=pl.CostEstimate(flops=20_000_000, bytes_accessed=10_000_000, transcendentals=0),
        name="norm",
    )(where, gain_column, *g, most, last)

    width = w_query.shape[1]
    hbm = pl.BlockSpec(memory_space=pl.ANY)
    n_first = NX * len(EARLY) + (NX - 1) * len(LATE)
    part = pl.pallas_call(
        first_kernel,
        out_shape=jax.ShapeDtypeStruct((LEN, 3 * width), F32),
        in_specs=[smem, vmem] + [hbm] * (NX + 1),
        out_specs=vmem,
        scratch_shapes=[
            pltpu.VMEM((n_first,) + weight.shape, BF),
            pltpu.SemaphoreType.DMA((3 * NX - 1,)),
        ],
        compiler_params=pltpu.CompilerParams(vmem_limit_bytes=54 << 20),
        cost_estimate=pl.CostEstimate(
            flops=2_200_000_000, bytes_accessed=12_000_000, transcendentals=0),
        name="first",
    )(where, normed, *early, *late[:NX - 1])

    half = jax.ShapeDtypeStruct((NY * SHARD, LEN), BF)
    half_tail = jax.ShapeDtypeStruct((NY * SHARD + TAIL, LEN), BF)
    context, keep_a, keep_b, give_a, give_b = pl.pallas_call(
        main_kernel,
        out_shape=(jax.ShapeDtypeStruct((LEN, width), BF), half, half_tail, half, half_tail),
        in_specs=[smem] + [vmem] * 8 + [hbm] * (4 + NX),
        out_specs=(vmem,) * 5,
        scratch_shapes=[
            pltpu.VMEM((NZ * NX,) + weight.shape, BF),
            pltpu.VMEM((len(LATE), BLOCK, LEN), BF),
            pltpu.VMEM((D, LEN), BF),
            pltpu.VMEM((LEN, 3 * width), F32),
            pltpu.VMEM((LEN, 3 * width), BF),
            pltpu.SemaphoreType.DMA((3 * NX + len(LATE) + 1,)),
        ],
        compiler_params=pltpu.CompilerParams(vmem_limit_bytes=54 << 20),
        cost_estimate=pl.CostEstimate(
            flops=3_000_000_000, bytes_accessed=20_000_000, transcendentals=131072),
        name="core",
    )(where, gain_column, stat, segment[None, :], segment[:, None], query_gain[None, :],
      key_gain[None, :], attn_cotangent, part, normed, packed, *early, *late)

    rows = NY * SHARD
    y_swap = functools.partial(
        lax.all_to_all, axis_name="y", split_axis=0, concat_axis=0, tiled=True)
    taken = lax.ppermute(give_b, "c", shift(NC, 1))
    tails = [a + b for a, b in zip(join_sums(keep_b[rows:]), join_sums(taken[rows:]))]
    both = (keep_b[:rows].astype(F32) + taken[:rows].astype(F32)).astype(BF)
    tail = jnp.broadcast_to(split_sums(*tails)[None], (NY, TAIL, LEN))
    got_b = y_swap(jnp.concatenate([both.reshape(NY, SHARD, LEN), tail], axis=1))
    taken = lax.ppermute(give_a, "c", shift(NC, 1))
    both = (keep_a.astype(F32) + taken.astype(F32)).astype(BF)
    got_a = y_swap(both.reshape(NY, SHARD, LEN))
    leave = jnp.sum(got_b[:, :SHARD].astype(F32), axis=0).astype(BF)
    sums = [jnp.sum(a, axis=0) for a in join_sums(got_b[:, SHARD:])]
    came = lax.ppermute(
        jnp.concatenate([leave, split_sums(*sums)], axis=0), "zh", shift(NH, 1))
    shard = jnp.sum(got_a.astype(F32), axis=0) + came[:SHARD].astype(F32)
    first, second = [a + b for a, b in zip(sums, join_sums(came[SHARD:]))]

    index = (y * NH + zh) * NC + c
    gain_here = lax.dynamic_slice_in_dim(ln_gain, index * SHARD, SHARD, 0)[:, None]
    mean, inverse = stat[0:1], stat[1:2]
    x_hat = (mine.astype(F32) - mean) * inverse
    grad = (shard * gain_here - first / D - x_hat * (second / D)) * inverse
    return context, grad.T.astype(BF)


def solution(mesh):
    fine = Mesh(mesh.devices.reshape(NZ, NX, NY, NH, NC), ("zl", "x", "y", "zh", "c"))
    dp, mp = ("zl", "x"), ("y", "zh", "c")
    placed = (
        P(dp, mp), P(dp), P(dp), P(), P(dp, mp), P(dp, mp), P(dp, mp), P(mp), P(mp), P(dp, mp),
    )
    return jax.shard_map(
        per_device,
        mesh=fine,
        in_specs=placed,
        out_specs=(P(dp, mp), P(dp, mp)),
        check_vma=False,
    )
```

```python
import functools
import math

import jax
import jax.numpy as jnp
from jax import lax
from jax.experimental import pallas as pl
from jax.experimental.pallas import tpu as pltpu
from jax.sharding import Mesh, PartitionSpec as P

D = 6144
DH = 128
LEN = 256
CAP = 16
NZ, NX, NY, NH, NC = 8, 4, 4, 2, 2
SHARD = D // (NY * NH * NC)
BLOCK = D // (NZ * NX)
EPSILON = 1e-06
NEGATIVE = -1e30
BF = jnp.bfloat16
F32 = jnp.float32
FOLD = [0, 2, 4, 6, 7, 5, 3, 1]
Z_RING = [(FOLD[i], FOLD[(i + 1) % NZ]) for i in range(NZ)]
Z_BACK = [(b, a) for a, b in Z_RING]
EARLY = (0, 1, -1, 2, -2)
FIRST = 1
LATE = (3, -3, 4)
TAIL = 16


def shift(n, k):
    return [(i, (i + k) % n) for i in range(n)]


def core_ring(n):
    return [(i * NC + k, (i + (1, n - 1)[k]) % n * NC + k) for i in range(n) for k in range(NC)]


def after(value, other):
    return value + other[(0,) * other.ndim] * 0


def contract(a, b, dim_a, dim_b):
    return lax.dot_general(
        a, b, (((dim_a,), (dim_b,)), ((), ())), preferred_element_type=F32
    )


def ring_source(place, core, steps, n):
    return lax.rem(place + jnp.where(core == 0, n - steps, steps), n)


def norm_kernel(where_ref, gain_ref, *rest):
    y, zh, c = where_ref[0], where_ref[1], where_ref[2]
    own, others = rest[:NY], rest[NY:NY + 2]
    normed_ref, packed_ref, stat_ref = rest[NY + 2:]
    blocks = []
    for steps in range(NY):
        for flip in range(NH):
            half = lax.rem(zh + flip, NH)
            there = ring_source(y, c, steps, NY) * NH + half
            blocks.append((own[steps], flip, there * NC + c))
            there = ring_source(y, 1 - c, steps, NY) * NH + half
            ref, i = (others[0], 2 * steps + flip) if steps < NY - 1 else (others[1], flip)
            blocks.append((ref, i, there * NC + (1 - c)))
    total = jnp.zeros((1, LEN), F32)
    for ref, i, _ in blocks:
        total = total + jnp.sum(ref[i].astype(F32), axis=0, keepdims=True)
    mean = total / D
    total = jnp.zeros((1, LEN), F32)
    for ref, i, _ in blocks:
        centred = ref[i].astype(F32) - mean
        total = total + jnp.sum(centred * centred, axis=0, keepdims=True)
    inverse = lax.rsqrt(total / D + EPSILON)
    stat_ref[0:1, :] = mean
    stat_ref[1:2, :] = inverse
    for ref, i, index in blocks:
        rows = pl.ds(pl.multiple_of(index * SHARD, SHARD), SHARD)
        value = ref[i]
        packed_ref[rows, :] = value
        normed_ref[rows, :] = (
            (value.astype(F32) - mean) * inverse * gain_ref[rows, :]
        ).astype(BF)


def row_norm(values_in):
    row_mean = jnp.mean(values_in, axis=-1, keepdims=True)
    centred = values_in - row_mean
    row_var = jnp.mean(centred * centred, axis=-1, keepdims=True)
    inverse = lax.rsqrt(row_var + EPSILON)
    return centred * inverse, inverse


def norm_back(grad_hat, scaled, inverse):
    first = jnp.mean(grad_hat, axis=-1, keepdims=True)
    second = jnp.mean(grad_hat * scaled, axis=-1, keepdims=True)
    return (grad_hat - first - scaled * second) * inverse


def weight_blocks(where_ref):
    c, zl, x = where_ref[2], where_ref[3], where_ref[4]
    position = jnp.where(lax.rem(zl, 2) == 0, zl // 2, 7 - zl // 2)
    found = []
    for steps in (EARLY[:FIRST], EARLY[FIRST:], LATE):
        for off in range(NX):
            x_from = ring_source(x, c, off, NX) if steps is LATE else off
            for step in steps:
                p = lax.rem(position - step + NZ, NZ)
                z_from = jnp.where(p < 4, 2 * p, 15 - 2 * p)
                found.append(z_from * NX + x_from)
    return found


def block_rows(block):
    return pl.ds(pl.multiple_of(block * BLOCK, BLOCK), BLOCK)


def load_weights(early_refs, late_refs, weight_ref, sems):
    sources = []
    for ref in early_refs:
        sources.extend((ref.at[off], ref.shape[1]) for off in range(NX))
    sources.extend((ref, ref.shape[0]) for ref in late_refs)
    copies = {}
    slot = 0
    for n, (source, size) in enumerate(sources):
        copies[slot] = pltpu.make_async_copy(
            source, weight_ref.at[slot:slot + size], sems.at[n])
        slot += size
    return copies


def first_kernel(where_ref, normed_ref, early0_ref, early1_ref, late0_ref, late1_ref, late2_ref,
                 acc_ref, weight_ref, sems):
    blocks = weight_blocks(where_ref)
    copies = load_weights(
        (early0_ref, early1_ref), (late0_ref, late1_ref, late2_ref), weight_ref, sems)
    for copy in copies.values():
        copy.start()
    for slot in range(weight_ref.shape[0]):
        if slot in copies:
            copies[slot].wait()
        part = contract(normed_ref[block_rows(blocks[slot]), :], weight_ref[slot], 0, 0)
        if slot == 0:
            acc_ref[...] = part
        else:
            acc_ref[...] += part


def main_kernel(where_ref, gain_ref, stat_ref, seg_row_ref, seg_col_ref, qgain_ref, kgain_ref,
                cot_ref, part_ref, normed_ref, packed_hbm, *rest):
    early_refs, late_refs, rest = rest[:2], rest[2:2 + NX], rest[2 + NX:]
    attn_ref, keep_a, keep_b, give_a, give_b = rest[:5]
    weight_ref, rows_ref, packed_ref, acc_ref, grad_ref, sems = rest[5:]
    zh, c = where_ref[1], where_ref[2]
    blocks = weight_blocks(where_ref)
    final = NZ * NX - len(LATE)

    arrived = load_weights(early_refs, late_refs, weight_ref, sems)
    last_copy = arrived.pop(final)
    last_copy.start()
    row_copies = [
        pltpu.make_async_copy(
            normed_ref.at[block_rows(blocks[final + j]), :], rows_ref.at[j], sems.at[3 * NX + j])
        for j in range(len(LATE))
    ]
    packed_copy = pltpu.make_async_copy(packed_hbm, packed_ref, sems.at[3 * NX + len(LATE)])
    for copy in row_copies + list(arrived.values()) + [packed_copy]:
        copy.start()

    last_copy.wait()
    for j, copy in enumerate(row_copies):
        copy.wait()
        part = contract(rows_ref[j], weight_ref[final + j], 0, 0)
        if j == 0:
            acc_ref[...] = part_ref[...] + part
        else:
            acc_ref[...] += part

    factor = 1.0 / math.sqrt(DH)
    same = seg_col_ref[...] == seg_row_ref[...]
    width = qgain_ref.shape[1]
    for h in range(width // DH):
        cols = slice(h * DH, (h + 1) * DH)
        qgain, kgain = qgain_ref[:, cols], kgain_ref[:, cols]
        query_hat, query_inv = row_norm(acc_ref[:, h * DH:(h + 1) * DH])
        key_hat, key_inv = row_norm(acc_ref[:, width + h * DH:width + (h + 1) * DH])
        value = acc_ref[:, 2 * width + h * DH:2 * width + (h + 1) * DH].astype(BF)
        query = (query_hat * qgain).astype(BF)
        key = (key_hat * kgain).astype(BF)
        cot = cot_ref[:, cols]
        scores = jnp.where(same, contract(query, key, 1, 1) * factor, NEGATIVE)
        exp_scores = jnp.exp(scores - jnp.max(scores, axis=-1, keepdims=True))
        prob = exp_scores / jnp.sum(exp_scores, axis=-1, keepdims=True)
        prob_half = prob.astype(BF)
        attn_ref[:, cols] = contract(prob_half, value, 1, 0).astype(BF)
        grad_prob = contract(cot, value, 1, 1)
        delta = jnp.sum(prob * grad_prob, axis=-1, keepdims=True)
        grad_score = (prob * (grad_prob - delta) * factor).astype(BF)
        query_side = contract(grad_score, key, 1, 0)
        key_side = contract(grad_score, query, 0, 0)
        grad_ref[:, h * DH:(h + 1) * DH] = norm_back(
            query_side * qgain, query_hat, query_inv).astype(BF)
        grad_ref[:, width + h * DH:width + (h + 1) * DH] = norm_back(
            key_side * kgain, key_hat, key_inv).astype(BF)
        grad_ref[:, 2 * width + h * DH:2 * width + (h + 1) * DH] = contract(
            prob_half, cot, 0, 0).astype(BF)

    mean, inverse = stat_ref[0:1, :], stat_ref[1:2, :]
    first = jnp.zeros((1, LEN), F32)
    second = jnp.zeros((1, LEN), F32)
    packed_copy.wait()
    for slot, block in enumerate(blocks):
        if slot in arrived:
            arrived[slot].wait()
        rows = block_rows(block)
        term = contract(weight_ref[slot], grad_ref[...], 1, 1).astype(BF)
        scaled = term.astype(F32) * gain_ref[rows, :]
        first = first + jnp.sum(scaled, axis=0, keepdims=True)
        second = second + jnp.sum(
            scaled * (packed_ref[rows, :].astype(F32) - mean), axis=0, keepdims=True)
        same_core = lax.rem(block // 2, NC) == c
        same_half = lax.rem(block // 4, NH) == zh
        target = (block // 8) * SHARD + lax.rem(block, 2) * BLOCK
        out = pl.ds(pl.multiple_of(target, BLOCK), BLOCK)
        for core_flag, half_flag, ref in (
            (True, True, keep_a), (True, False, keep_b),
            (False, True, give_a), (False, False, give_b),
        ):
            @pl.when(jnp.logical_and(same_core == core_flag, same_half == half_flag))
            def _(ref=ref):
                ref[out, :] = term

    sums = split_sums(first, second * inverse)
    keep_b[NY * SHARD:, :] = sums
    give_b[NY * SHARD:, :] = sums


def split_sums(first, second):
    rows = []
    for value in (first, second):
        for _ in range(3):
            piece = value.astype(BF)
            rows.append(piece.astype(F32))
            value = value - piece.astype(F32)
    rows.append(jnp.zeros((TAIL - len(rows), LEN), F32))
    return jnp.concatenate(rows, axis=0).astype(BF)


def join_sums(tail):
    tail = tail.astype(F32)
    return (
        tail[..., 0:1, :] + tail[..., 1:2, :] + tail[..., 2:3, :],
        tail[..., 3:4, :] + tail[..., 4:5, :] + tail[..., 5:6, :],
    )


def send_packets(patches, destination):
    rows = patches.shape[0]
    n_groups = NZ * NX
    owners = destination // LEN
    offsets = destination % LEN
    one_hot = (owners[:, None] == jnp.arange(n_groups)[None, :]).astype(BF)
    index = jnp.arange(rows)
    strict = (index[:, None] > index[None, :]).astype(BF)
    earlier = jnp.dot(strict, one_hot, preferred_element_type=F32)
    rank = jnp.sum(earlier * one_hot.astype(F32), axis=1).astype(jnp.int32)
    position = owners * CAP + rank
    placing = jnp.arange(n_groups * CAP)[:, None] == position[None, :]
    sent = jnp.dot(placing.astype(BF), patches, preferred_element_type=F32).astype(BF)
    places = jnp.sum(jnp.where(placing, offsets[None, :] + 1, 0), axis=1)
    places = places.reshape(n_groups, 1, CAP).astype(BF)
    places = jnp.pad(places, ((0, 0), (0, 7), (0, 128 - CAP)))
    blocks = [
        sent[:, i:i + 128].reshape(n_groups, CAP, 128) for i in range(0, sent.shape[1], 128)
    ]
    return jnp.concatenate(blocks + [places], axis=1)


def unpack(got):
    n_groups = got.shape[0]
    n_blocks = (got.shape[1] - 8) // CAP
    places = got[:, n_blocks * CAP, :CAP].astype(jnp.int32).reshape(n_groups * CAP) - 1
    chosen = (places[:, None] == jnp.arange(LEN)[None, :]).astype(BF)
    out = [
        contract(
            got[:, i * CAP:(i + 1) * CAP].reshape(n_groups * CAP, 128), chosen, 0, 0
        ).astype(BF)
        for i in range(n_blocks)
    ]
    return jnp.concatenate(out, axis=0)


def per_device(patches, destination, segment, ln_gain, w_query, w_key, w_value,
               query_gain, key_gain, attn_cotangent):
    y, zh, c = lax.axis_index("y"), lax.axis_index("zh"), lax.axis_index("c")
    zl, x = lax.axis_index("zl"), lax.axis_index("x")
    where = jnp.stack([y, zh, c, zl, x]).astype(jnp.int32)
    gain_column = ln_gain[:, None]

    weight = jnp.concatenate([w_query, w_key, w_value], axis=1)
    packets = send_packets(patches, destination)

    x_ring = functools.partial(lax.ppermute, axis_name=("x", "c"), perm=core_ring(NX))
    y_ring = functools.partial(lax.ppermute, axis_name=("y", "c"), perm=core_ring(NY))
    got = lax.all_to_all(packets, ("zl", "x"), split_axis=0, concat_axis=0, tiled=True)
    mine = unpack(got)
    partner = lax.ppermute(mine, "zh", shift(NH, 1))
    g = [jnp.stack([mine, partner])]
    g.append(y_ring(g[0]))
    wait_for = {2: got, 3: partner, 4: g[1]}
    z = {0: weight}
    for step in (1, 2, 3, 4):
        block = z[step - 1]
        if step in wait_for:
            block = after(block, wait_for[step])
        z[step] = lax.ppermute(block, "zl", Z_RING)
        if step < 4:
            z[-step] = lax.ppermute(z[1 - step], "zl", Z_BACK)
    early = []
    for steps in (EARLY[:FIRST], EARLY[FIRST:]):
        joined = lax.all_gather(
            jnp.concatenate([after(z[n], partner) if n == -1 else z[n] for n in steps]),
            "x", axis=0, tiled=True)
        early.append(joined.reshape((NX, len(steps)) + weight.shape))
    late = [jnp.stack([z[n] for n in LATE])]
    for _ in range(NX - 1):
        late.append(x_ring(late[-1]))

    for _ in range(NY - 2):
        g.append(y_ring(g[-1]))
    most = lax.ppermute(jnp.concatenate(g[:3]), "c", shift(NC, 1))
    last = lax.ppermute(g[3], "c", shift(NC, 1))

    vmem = pl.BlockSpec(memory_space=pltpu.VMEM)
    smem = pl.BlockSpec(memory_space=pltpu.SMEM)
    normed, packed, stat = pl.pallas_call(
        norm_kernel,
        out_shape=(
            jax.ShapeDtypeStruct((D, LEN), BF),
            jax.ShapeDtypeStruct((D, LEN), BF),
            jax.ShapeDtypeStruct((2, LEN), F32),
        ),
        in_specs=[smem] + [vmem] * 7,
        out_specs=(vmem, vmem, vmem),
        compiler_params=pltpu.CompilerParams(vmem_limit_bytes=32 << 20),
        cost_estimate=pl.CostEstimate(flops=20_000_000, bytes_accessed=10_000_000, transcendentals=0),
        name="norm",
    )(where, gain_column, *g, most, last)

    width = w_query.shape[1]
    hbm = pl.BlockSpec(memory_space=pl.ANY)
    n_first = NX * len(EARLY) + (NX - 1) * len(LATE)
    part = pl.pallas_call(
        first_kernel,
        out_shape=jax.ShapeDtypeStruct((LEN, 3 * width), F32),
        in_specs=[smem, vmem] + [hbm] * (NX + 1),
        out_specs=vmem,
        scratch_shapes=[
            pltpu.VMEM((n_first,) + weight.shape, BF),
            pltpu.SemaphoreType.DMA((3 * NX - 1,)),
        ],
        compiler_params=pltpu.CompilerParams(vmem_limit_bytes=54 << 20),
        cost_estimate=pl.CostEstimate(
            flops=2_200_000_000, bytes_accessed=12_000_000, transcendentals=0),
        name="first",
    )(where, normed, *early, *late[:NX - 1])

    half = jax.ShapeDtypeStruct((NY * SHARD, LEN), BF)
    half_tail = jax.ShapeDtypeStruct((NY * SHARD + TAIL, LEN), BF)
    context, keep_a, keep_b, give_a, give_b = pl.pallas_call(
        main_kernel,
        out_shape=(jax.ShapeDtypeStruct((LEN, width), BF), half, half_tail, half, half_tail),
        in_specs=[smem] + [vmem] * 8 + [hbm] * (4 + NX),
        out_specs=(vmem,) * 5,
        scratch_shapes=[
            pltpu.VMEM((NZ * NX,) + weight.shape, BF),
            pltpu.VMEM((len(LATE), BLOCK, LEN), BF),
            pltpu.VMEM((D, LEN), BF),
            pltpu.VMEM((LEN, 3 * width), F32),
            pltpu.VMEM((LEN, 3 * width), BF),
            pltpu.SemaphoreType.DMA((3 * NX + len(LATE) + 1,)),
        ],
        compiler_params=pltpu.CompilerParams(vmem_limit_bytes=36 << 20),
        cost_estimate=pl.CostEstimate(
            flops=3_000_000_000, bytes_accessed=20_000_000, transcendentals=131072),
        name="core",
    )(where, gain_column, stat, segment[None, :], segment[:, None], query_gain[None, :],
      key_gain[None, :], attn_cotangent, part, normed, packed, *early, *late)

    rows = NY * SHARD
    y_swap = functools.partial(
        lax.all_to_all, axis_name="y", split_axis=0, concat_axis=0, tiled=True)
    taken = lax.ppermute(give_b, "c", shift(NC, 1))
    tails = [a + b for a, b in zip(join_sums(keep_b[rows:]), join_sums(taken[rows:]))]
    both = (keep_b[:rows].astype(F32) + taken[:rows].astype(F32)).astype(BF)
    tail = jnp.broadcast_to(split_sums(*tails)[None], (NY, TAIL, LEN))
    got_b = y_swap(jnp.concatenate([both.reshape(NY, SHARD, LEN), tail], axis=1))
    taken = lax.ppermute(give_a, "c", shift(NC, 1))
    both = (keep_a.astype(F32) + taken.astype(F32)).astype(BF)
    got_a = y_swap(both.reshape(NY, SHARD, LEN))
    leave = jnp.sum(got_b[:, :SHARD].astype(F32), axis=0).astype(BF)
    sums = [jnp.sum(a, axis=0) for a in join_sums(got_b[:, SHARD:])]
    came = lax.ppermute(
        jnp.concatenate([leave, split_sums(*sums)], axis=0), "zh", shift(NH, 1))
    shard = jnp.sum(got_a.astype(F32), axis=0) + came[:SHARD].astype(F32)
    first, second = [a + b for a, b in zip(sums, join_sums(came[SHARD:]))]

    index = (y * NH + zh) * NC + c
    gain_here = lax.dynamic_slice_in_dim(ln_gain, index * SHARD, SHARD, 0)[:, None]
    mean, inverse = stat[0:1], stat[1:2]
    x_hat = (mine.astype(F32) - mean) * inverse
    grad = (shard * gain_here - first / D - x_hat * (second / D)) * inverse
    return context, grad.T.astype(BF)


def solution(mesh):
    fine = Mesh(mesh.devices.reshape(NZ, NX, NY, NH, NC), ("zl", "x", "y", "zh", "c"))
    dp, mp = ("zl", "x"), ("y", "zh", "c")
    placed = (
        P(dp, mp), P(dp), P(dp), P(), P(dp, mp), P(dp, mp), P(dp, mp), P(mp), P(mp), P(dp, mp),
    )
    return jax.shard_map(
        per_device,
        mesh=fine,
        in_specs=placed,
        out_specs=(P(dp, mp), P(dp, mp)),
        check_vma=False,
    )
```

```python
import functools
import math

import jax
import jax.numpy as jnp
from jax import lax
from jax.experimental import pallas as pl
from jax.experimental.pallas import tpu as pltpu
from jax.sharding import Mesh, PartitionSpec as P

D = 6144
DH = 128
LEN = 256
CAP = 16
NZ, NX, NY, NH, NC = 8, 4, 4, 2, 2
SHARD = D // (NY * NH * NC)
BLOCK = D // (NZ * NX)
EPSILON = 1e-06
NEGATIVE = -1e30
BF = jnp.bfloat16
F32 = jnp.float32
FOLD = [0, 2, 4, 6, 7, 5, 3, 1]
Z_RING = [(FOLD[i], FOLD[(i + 1) % NZ]) for i in range(NZ)]
Z_BACK = [(b, a) for a, b in Z_RING]
EARLY = ((0,), (1, -1), (2, -2))
LATE = (3, -3, 4)
TAIL = 16


def shift(n, k):
    return [(i, (i + k) % n) for i in range(n)]


def core_ring(n):
    return [(i * NC + k, (i + (1, n - 1)[k]) % n * NC + k) for i in range(n) for k in range(NC)]


def after(value, other):
    return value + other[(0,) * other.ndim] * 0


def contract(a, b, dim_a, dim_b):
    return lax.dot_general(
        a, b, (((dim_a,), (dim_b,)), ((), ())), preferred_element_type=F32
    )


def ring_source(place, core, steps, n):
    return lax.rem(place + jnp.where(core == 0, n - steps, steps), n)


def norm_kernel(where_ref, gain_ref, *rest):
    y, zh, c = where_ref[0], where_ref[1], where_ref[2]
    own, others = rest[:NY], rest[NY:NY + 2]
    normed_ref, packed_ref, stat_ref = rest[NY + 2:]
    blocks = []
    for steps in range(NY):
        for flip in range(NH):
            half = lax.rem(zh + flip, NH)
            there = ring_source(y, c, steps, NY) * NH + half
            blocks.append((own[steps], flip, there * NC + c))
            there = ring_source(y, 1 - c, steps, NY) * NH + half
            ref, i = (others[0], 2 * steps + flip) if steps < NY - 1 else (others[1], flip)
            blocks.append((ref, i, there * NC + (1 - c)))
    total = jnp.zeros((1, LEN), F32)
    for ref, i, _ in blocks:
        total = total + jnp.sum(ref[i].astype(F32), axis=0, keepdims=True)
    mean = total / D
    total = jnp.zeros((1, LEN), F32)
    for ref, i, _ in blocks:
        centred = ref[i].astype(F32) - mean
        total = total + jnp.sum(centred * centred, axis=0, keepdims=True)
    inverse = lax.rsqrt(total / D + EPSILON)
    stat_ref[0:1, :] = mean
    stat_ref[1:2, :] = inverse
    for ref, i, index in blocks:
        rows = pl.ds(pl.multiple_of(index * SHARD, SHARD), SHARD)
        value = ref[i]
        packed_ref[rows, :] = value
        normed_ref[rows, :] = (
            (value.astype(F32) - mean) * inverse * gain_ref[rows, :]
        ).astype(BF)


def row_norm(values_in):
    row_mean = jnp.mean(values_in, axis=-1, keepdims=True)
    centred = values_in - row_mean
    row_var = jnp.mean(centred * centred, axis=-1, keepdims=True)
    inverse = lax.rsqrt(row_var + EPSILON)
    return centred * inverse, inverse


def norm_back(grad_hat, scaled, inverse):
    first = jnp.mean(grad_hat, axis=-1, keepdims=True)
    second = jnp.mean(grad_hat * scaled, axis=-1, keepdims=True)
    return (grad_hat - first - scaled * second) * inverse


def weight_blocks(where_ref):
    c, zl, x = where_ref[2], where_ref[3], where_ref[4]
    position = jnp.where(lax.rem(zl, 2) == 0, zl // 2, 7 - zl // 2)
    found = []
    for steps in EARLY + (LATE,):
        for off in range(NX):
            x_from = ring_source(x, c, off, NX) if steps is LATE else off
            for step in steps:
                p = lax.rem(position - step + NZ, NZ)
                z_from = jnp.where(p < 4, 2 * p, 15 - 2 * p)
                found.append(z_from * NX + x_from)
    return found


def block_rows(block):
    return pl.ds(pl.multiple_of(block * BLOCK, BLOCK), BLOCK)


def load_weights(early_refs, late_refs, weight_ref, sems):
    sources = []
    for ref in early_refs:
        sources.extend((ref.at[off], ref.shape[1]) for off in range(NX))
    sources.extend((ref, ref.shape[0]) for ref in late_refs)
    copies = {}
    slot = 0
    for n, (source, size) in enumerate(sources):
        copies[slot] = pltpu.make_async_copy(
            source, weight_ref.at[slot:slot + size], sems.at[n])
        slot += size
    return copies


def first_kernel(where_ref, normed_ref, *rest):
    early_refs, late_refs = rest[:len(EARLY)], rest[len(EARLY):len(EARLY) + NX - 1]
    acc_ref, weight_ref, sems = rest[len(EARLY) + NX - 1:]
    blocks = weight_blocks(where_ref)
    copies = load_weights(early_refs, late_refs, weight_ref, sems)
    for copy in copies.values():
        copy.start()
    for slot in range(weight_ref.shape[0]):
        if slot in copies:
            copies[slot].wait()
        part = contract(normed_ref[block_rows(blocks[slot]), :], weight_ref[slot], 0, 0)
        if slot == 0:
            acc_ref[...] = part
        else:
            acc_ref[...] += part


def main_kernel(where_ref, gain_ref, stat_ref, seg_row_ref, seg_col_ref, qgain_ref, kgain_ref,
                cot_ref, part_ref, normed_ref, packed_hbm, *rest):
    n_early = len(EARLY)
    early_refs, late_refs = rest[:n_early], rest[n_early:n_early + NX]
    rest = rest[n_early + NX:]
    n_copies = (n_early + 1) * NX
    attn_ref, keep_a, keep_b, give_a, give_b = rest[:5]
    weight_ref, rows_ref, packed_ref, acc_ref, grad_ref, sems = rest[5:]
    zh, c = where_ref[1], where_ref[2]
    blocks = weight_blocks(where_ref)
    final = NZ * NX - len(LATE)

    arrived = load_weights(early_refs, late_refs, weight_ref, sems)
    last_copy = arrived.pop(final)
    last_copy.start()
    row_copies = [
        pltpu.make_async_copy(
            normed_ref.at[block_rows(blocks[final + j]), :], rows_ref.at[j], sems.at[n_copies + j])
        for j in range(len(LATE))
    ]
    packed_copy = pltpu.make_async_copy(packed_hbm, packed_ref, sems.at[n_copies + len(LATE)])
    for copy in row_copies + list(arrived.values()) + [packed_copy]:
        copy.start()

    last_copy.wait()
    for j, copy in enumerate(row_copies):
        copy.wait()
        part = contract(rows_ref[j], weight_ref[final + j], 0, 0)
        if j == 0:
            acc_ref[...] = part_ref[...] + part
        else:
            acc_ref[...] += part

    factor = 1.0 / math.sqrt(DH)
    same = seg_col_ref[...] == seg_row_ref[...]
    width = qgain_ref.shape[1]
    for h in range(width // DH):
        cols = slice(h * DH, (h + 1) * DH)
        qgain, kgain = qgain_ref[:, cols], kgain_ref[:, cols]
        query_hat, query_inv = row_norm(acc_ref[:, h * DH:(h + 1) * DH])
        key_hat, key_inv = row_norm(acc_ref[:, width + h * DH:width + (h + 1) * DH])
        value = acc_ref[:, 2 * width + h * DH:2 * width + (h + 1) * DH].astype(BF)
        query = (query_hat * qgain).astype(BF)
        key = (key_hat * kgain).astype(BF)
        cot = cot_ref[:, cols]
        scores = jnp.where(same, contract(query, key, 1, 1) * factor, NEGATIVE)
        exp_scores = jnp.exp(scores - jnp.max(scores, axis=-1, keepdims=True))
        prob = exp_scores / jnp.sum(exp_scores, axis=-1, keepdims=True)
        prob_half = prob.astype(BF)
        attn_ref[:, cols] = contract(prob_half, value, 1, 0).astype(BF)
        grad_prob = contract(cot, value, 1, 1)
        delta = jnp.sum(prob * grad_prob, axis=-1, keepdims=True)
        grad_score = (prob * (grad_prob - delta) * factor).astype(BF)
        query_side = contract(grad_score, key, 1, 0)
        key_side = contract(grad_score, query, 0, 0)
        grad_ref[:, h * DH:(h + 1) * DH] = norm_back(
            query_side * qgain, query_hat, query_inv).astype(BF)
        grad_ref[:, width + h * DH:width + (h + 1) * DH] = norm_back(
            key_side * kgain, key_hat, key_inv).astype(BF)
        grad_ref[:, 2 * width + h * DH:2 * width + (h + 1) * DH] = contract(
            prob_half, cot, 0, 0).astype(BF)

    mean, inverse = stat_ref[0:1, :], stat_ref[1:2, :]
    first = jnp.zeros((1, LEN), F32)
    second = jnp.zeros((1, LEN), F32)
    packed_copy.wait()
    for slot, block in enumerate(blocks):
        if slot in arrived:
            arrived[slot].wait()
        rows = block_rows(block)
        term = contract(weight_ref[slot], grad_ref[...], 1, 1).astype(BF)
        scaled = term.astype(F32) * gain_ref[rows, :]
        first = first + jnp.sum(scaled, axis=0, keepdims=True)
        second = second + jnp.sum(
            scaled * (packed_ref[rows, :].astype(F32) - mean), axis=0, keepdims=True)
        same_core = lax.rem(block // 2, NC) == c
        same_half = lax.rem(block // 4, NH) == zh
        target = (block // 8) * SHARD + lax.rem(block, 2) * BLOCK
        out = pl.ds(pl.multiple_of(target, BLOCK), BLOCK)
        for core_flag, half_flag, ref in (
            (True, True, keep_a), (True, False, keep_b),
            (False, True, give_a), (False, False, give_b),
        ):
            @pl.when(jnp.logical_and(same_core == core_flag, same_half == half_flag))
            def _(ref=ref):
                ref[out, :] = term

    sums = split_sums(first, second * inverse)
    keep_b[NY * SHARD:, :] = sums
    give_b[NY * SHARD:, :] = sums


def split_sums(first, second):
    rows = []
    for value in (first, second):
        for _ in range(3):
            piece = value.astype(BF)
            rows.append(piece.astype(F32))
            value = value - piece.astype(F32)
    rows.append(jnp.zeros((TAIL - len(rows), LEN), F32))
    return jnp.concatenate(rows, axis=0).astype(BF)


def join_sums(tail):
    tail = tail.astype(F32)
    return (
        tail[..., 0:1, :] + tail[..., 1:2, :] + tail[..., 2:3, :],
        tail[..., 3:4, :] + tail[..., 4:5, :] + tail[..., 5:6, :],
    )


def send_packets(patches, destination):
    rows = patches.shape[0]
    n_groups = NZ * NX
    owners = destination // LEN
    offsets = destination % LEN
    one_hot = (owners[:, None] == jnp.arange(n_groups)[None, :]).astype(BF)
    index = jnp.arange(rows)
    strict = (index[:, None] > index[None, :]).astype(BF)
    earlier = jnp.dot(strict, one_hot, preferred_element_type=F32)
    rank = jnp.sum(earlier * one_hot.astype(F32), axis=1).astype(jnp.int32)
    position = owners * CAP + rank
    placing = jnp.arange(n_groups * CAP)[:, None] == position[None, :]
    sent = jnp.dot(placing.astype(BF), patches, preferred_element_type=F32).astype(BF)
    places = jnp.sum(jnp.where(placing, offsets[None, :] + 1, 0), axis=1)
    places = places.reshape(n_groups, 1, CAP).astype(BF)
    places = jnp.pad(places, ((0, 0), (0, 7), (0, 128 - CAP)))
    blocks = [
        sent[:, i:i + 128].reshape(n_groups, CAP, 128) for i in range(0, sent.shape[1], 128)
    ]
    return jnp.concatenate(blocks + [places], axis=1)


def unpack(got):
    n_groups = got.shape[0]
    n_blocks = (got.shape[1] - 8) // CAP
    places = got[:, n_blocks * CAP, :CAP].astype(jnp.int32).reshape(n_groups * CAP) - 1
    chosen = (places[:, None] == jnp.arange(LEN)[None, :]).astype(BF)
    out = [
        contract(
            got[:, i * CAP:(i + 1) * CAP].reshape(n_groups * CAP, 128), chosen, 0, 0
        ).astype(BF)
        for i in range(n_blocks)
    ]
    return jnp.concatenate(out, axis=0)


def per_device(patches, destination, segment, ln_gain, w_query, w_key, w_value,
               query_gain, key_gain, attn_cotangent):
    y, zh, c = lax.axis_index("y"), lax.axis_index("zh"), lax.axis_index("c")
    zl, x = lax.axis_index("zl"), lax.axis_index("x")
    where = jnp.stack([y, zh, c, zl, x]).astype(jnp.int32)
    gain_column = ln_gain[:, None]

    weight = jnp.concatenate([w_query, w_key, w_value], axis=1)
    packets = send_packets(patches, destination)

    x_ring = functools.partial(lax.ppermute, axis_name=("x", "c"), perm=core_ring(NX))
    y_ring = functools.partial(lax.ppermute, axis_name=("y", "c"), perm=core_ring(NY))
    got = lax.all_to_all(packets, ("zl", "x"), split_axis=0, concat_axis=0, tiled=True)
    mine = unpack(got)
    partner = lax.ppermute(mine, "zh", shift(NH, 1))
    g = [jnp.stack([mine, partner])]
    g.append(y_ring(g[0]))
    wait_for = {2: got, 3: partner, 4: g[1]}
    z = {0: weight}
    for step in (1, 2, 3, 4):
        block = z[step - 1]
        if step in wait_for:
            block = after(block, wait_for[step])
        z[step] = lax.ppermute(block, "zl", Z_RING)
        if step < 4:
            z[-step] = lax.ppermute(z[1 - step], "zl", Z_BACK)
    early = []
    for steps in EARLY:
        joined = lax.all_gather(
            jnp.concatenate([after(z[n], partner) if n == -2 else z[n] for n in steps]),
            "x", axis=0, tiled=True)
        early.append(joined.reshape((NX, len(steps)) + weight.shape))
    for _ in range(NY - 2):
        g.append(y_ring(g[-1]))
    late = [jnp.stack([after(z[n], g[3]) if n < 0 else z[n] for n in LATE])]
    for _ in range(NX - 1):
        late.append(x_ring(late[-1]))
    most = lax.ppermute(jnp.concatenate(g[:3]), "c", shift(NC, 1))
    last = lax.ppermute(g[3], "c", shift(NC, 1))

    vmem = pl.BlockSpec(memory_space=pltpu.VMEM)
    smem = pl.BlockSpec(memory_space=pltpu.SMEM)
    normed, packed, stat = pl.pallas_call(
        norm_kernel,
        out_shape=(
            jax.ShapeDtypeStruct((D, LEN), BF),
            jax.ShapeDtypeStruct((D, LEN), BF),
            jax.ShapeDtypeStruct((2, LEN), F32),
        ),
        in_specs=[smem] + [vmem] * 7,
        out_specs=(vmem, vmem, vmem),
        compiler_params=pltpu.CompilerParams(vmem_limit_bytes=32 << 20),
        cost_estimate=pl.CostEstimate(flops=20_000_000, bytes_accessed=10_000_000, transcendentals=0),
        name="norm",
    )(where, gain_column, *g, most, last)

    width = w_query.shape[1]
    hbm = pl.BlockSpec(memory_space=pl.ANY)
    n_first = NZ * NX - len(LATE)
    part = pl.pallas_call(
        first_kernel,
        out_shape=jax.ShapeDtypeStruct((LEN, 3 * width), F32),
        in_specs=[smem, vmem] + [hbm] * (len(EARLY) + NX - 1),
        out_specs=vmem,
        scratch_shapes=[
            pltpu.VMEM((n_first,) + weight.shape, BF),
            pltpu.SemaphoreType.DMA(((len(EARLY) + 1) * NX - 1,)),
        ],
        compiler_params=pltpu.CompilerParams(vmem_limit_bytes=54 << 20),
        cost_estimate=pl.CostEstimate(
            flops=2_200_000_000, bytes_accessed=12_000_000, transcendentals=0),
        name="first",
    )(where, normed, *early, *late[:NX - 1])

    half = jax.ShapeDtypeStruct((NY * SHARD, LEN), BF)
    half_tail = jax.ShapeDtypeStruct((NY * SHARD + TAIL, LEN), BF)
    context, keep_a, keep_b, give_a, give_b = pl.pallas_call(
        main_kernel,
        out_shape=(jax.ShapeDtypeStruct((LEN, width), BF), half, half_tail, half, half_tail),
        in_specs=[smem] + [vmem] * 8 + [hbm] * (2 + len(EARLY) + NX),
        out_specs=(vmem,) * 5,
        scratch_shapes=[
            pltpu.VMEM((NZ * NX,) + weight.shape, BF),
            pltpu.VMEM((len(LATE), BLOCK, LEN), BF),
            pltpu.VMEM((D, LEN), BF),
            pltpu.VMEM((LEN, 3 * width), F32),
            pltpu.VMEM((LEN, 3 * width), BF),
            pltpu.SemaphoreType.DMA(((len(EARLY) + 1) * NX + len(LATE) + 1,)),
        ],
        compiler_params=pltpu.CompilerParams(vmem_limit_bytes=36 << 20),
        cost_estimate=pl.CostEstimate(
            flops=3_000_000_000, bytes_accessed=20_000_000, transcendentals=131072),
        name="core",
    )(where, gain_column, stat, segment[None, :], segment[:, None], query_gain[None, :],
      key_gain[None, :], attn_cotangent, part, normed, packed, *early, *late)

    rows = NY * SHARD
    y_swap = functools.partial(
        lax.all_to_all, axis_name="y", split_axis=0, concat_axis=0, tiled=True)
    taken = lax.ppermute(give_b, "c", shift(NC, 1))
    tails = [a + b for a, b in zip(join_sums(keep_b[rows:]), join_sums(taken[rows:]))]
    both = (keep_b[:rows].astype(F32) + taken[:rows].astype(F32)).astype(BF)
    tail = jnp.broadcast_to(split_sums(*tails)[None], (NY, TAIL, LEN))
    got_b = y_swap(jnp.concatenate([both.reshape(NY, SHARD, LEN), tail], axis=1))
    taken = lax.ppermute(give_a, "c", shift(NC, 1))
    both = (keep_a.astype(F32) + taken.astype(F32)).astype(BF)
    got_a = y_swap(both.reshape(NY, SHARD, LEN))
    leave = jnp.sum(got_b[:, :SHARD].astype(F32), axis=0).astype(BF)
    sums = [jnp.sum(a, axis=0) for a in join_sums(got_b[:, SHARD:])]
    came = lax.ppermute(
        jnp.concatenate([leave, split_sums(*sums)], axis=0), "zh", shift(NH, 1))
    shard = jnp.sum(got_a.astype(F32), axis=0) + came[:SHARD].astype(F32)
    first, second = [a + b for a, b in zip(sums, join_sums(came[SHARD:]))]

    index = (y * NH + zh) * NC + c
    gain_here = lax.dynamic_slice_in_dim(ln_gain, index * SHARD, SHARD, 0)[:, None]
    mean, inverse = stat[0:1], stat[1:2]
    x_hat = (mine.astype(F32) - mean) * inverse
    grad = (shard * gain_here - first / D - x_hat * (second / D)) * inverse
    return context, grad.T.astype(BF)


def solution(mesh):
    fine = Mesh(mesh.devices.reshape(NZ, NX, NY, NH, NC), ("zl", "x", "y", "zh", "c"))
    dp, mp = ("zl", "x"), ("y", "zh", "c")
    placed = (
        P(dp, mp), P(dp), P(dp), P(), P(dp, mp), P(dp, mp), P(dp, mp), P(mp), P(mp), P(dp, mp),
    )
    return jax.shard_map(
        per_device,
        mesh=fine,
        in_specs=placed,
        out_specs=(P(dp, mp), P(dp, mp)),
        check_vma=False,
    )
```

```python
import functools
import math

import jax
import jax.numpy as jnp
from jax import lax
from jax.experimental import pallas as pl
from jax.experimental.pallas import tpu as pltpu
from jax.sharding import Mesh, PartitionSpec as P

D = 6144
DH = 128
LEN = 256
CAP = 16
NZ, NX, NY, NH, NC = 8, 4, 4, 2, 2
SHARD = D // (NY * NH * NC)
BLOCK = D // (NZ * NX)
EPSILON = 1e-06
NEGATIVE = -1e30
BF = jnp.bfloat16
F32 = jnp.float32
FOLD = [0, 2, 4, 6, 7, 5, 3, 1]
Z_RING = [(FOLD[i], FOLD[(i + 1) % NZ]) for i in range(NZ)]
Z_BACK = [(b, a) for a, b in Z_RING]
EARLY = ((0,), (1, -1), (2, -2))
LATE = (3, -3, 4)
TAIL = 16


def shift(n, k):
    return [(i, (i + k) % n) for i in range(n)]


def core_ring(n):
    return [(i * NC + k, (i + (1, n - 1)[k]) % n * NC + k) for i in range(n) for k in range(NC)]


def after(value, other):
    return value + other[(0,) * other.ndim] * 0


def contract(a, b, dim_a, dim_b):
    return lax.dot_general(
        a, b, (((dim_a,), (dim_b,)), ((), ())), preferred_element_type=F32
    )


def ring_source(place, core, steps, n):
    return lax.rem(place + jnp.where(core == 0, n - steps, steps), n)


def norm_kernel(where_ref, gain_ref, *rest):
    y, zh, c = where_ref[0], where_ref[1], where_ref[2]
    own, others = rest[:NY], rest[NY:NY + 2]
    normed_ref, packed_ref, stat_ref = rest[NY + 2:]
    blocks = []
    for steps in range(NY):
        for flip in range(NH):
            half = lax.rem(zh + flip, NH)
            there = ring_source(y, c, steps, NY) * NH + half
            blocks.append((own[steps], flip, there * NC + c))
            there = ring_source(y, 1 - c, steps, NY) * NH + half
            ref, i = (others[0], 2 * steps + flip) if steps < NY - 1 else (others[1], flip)
            blocks.append((ref, i, there * NC + (1 - c)))
    total = jnp.zeros((1, LEN), F32)
    for ref, i, _ in blocks:
        total = total + jnp.sum(ref[i].astype(F32), axis=0, keepdims=True)
    mean = total / D
    total = jnp.zeros((1, LEN), F32)
    for ref, i, _ in blocks:
        centred = ref[i].astype(F32) - mean
        total = total + jnp.sum(centred * centred, axis=0, keepdims=True)
    inverse = lax.rsqrt(total / D + EPSILON)
    stat_ref[0:1, :] = mean
    stat_ref[1:2, :] = inverse
    for ref, i, index in blocks:
        rows = pl.ds(pl.multiple_of(index * SHARD, SHARD), SHARD)
        value = ref[i]
        packed_ref[rows, :] = value
        normed_ref[rows, :] = (
            (value.astype(F32) - mean) * inverse * gain_ref[rows, :]
        ).astype(BF)


def row_norm(values_in):
    row_mean = jnp.mean(values_in, axis=-1, keepdims=True)
    centred = values_in - row_mean
    row_var = jnp.mean(centred * centred, axis=-1, keepdims=True)
    inverse = lax.rsqrt(row_var + EPSILON)
    return centred * inverse, inverse


def norm_back(grad_hat, scaled, inverse):
    first = jnp.mean(grad_hat, axis=-1, keepdims=True)
    second = jnp.mean(grad_hat * scaled, axis=-1, keepdims=True)
    return (grad_hat - first - scaled * second) * inverse


def weight_blocks(where_ref):
    c, zl, x = where_ref[2], where_ref[3], where_ref[4]
    position = jnp.where(lax.rem(zl, 2) == 0, zl // 2, 7 - zl // 2)
    found = []
    for steps in EARLY + (LATE,):
        for off in range(NX):
            x_from = ring_source(x, c, off, NX) if steps is LATE else off
            for step in steps:
                p = lax.rem(position - step + NZ, NZ)
                z_from = jnp.where(p < 4, 2 * p, 15 - 2 * p)
                found.append(z_from * NX + x_from)
    return found


def block_rows(block):
    return pl.ds(pl.multiple_of(block * BLOCK, BLOCK), BLOCK)


def load_weights(early_refs, late_refs, weight_ref, sems):
    sources = []
    for ref in early_refs:
        sources.extend((ref.at[off], ref.shape[1]) for off in range(NX))
    sources.extend((ref, ref.shape[0]) for ref in late_refs)
    copies = {}
    slot = 0
    for n, (source, size) in enumerate(sources):
        copies[slot] = pltpu.make_async_copy(
            source, weight_ref.at[slot:slot + size], sems.at[n])
        slot += size
    return copies


def first_kernel(where_ref, normed_ref, *rest):
    early_refs, late_refs = rest[:len(EARLY)], rest[len(EARLY):len(EARLY) + NX - 1]
    acc_ref, weight_ref, sems = rest[len(EARLY) + NX - 1:]
    blocks = weight_blocks(where_ref)
    copies = load_weights(early_refs, late_refs, weight_ref, sems)
    for copy in copies.values():
        copy.start()
    for slot in range(weight_ref.shape[0]):
        if slot in copies:
            copies[slot].wait()
        part = contract(normed_ref[block_rows(blocks[slot]), :], weight_ref[slot], 0, 0)
        if slot == 0:
            acc_ref[...] = part
        else:
            acc_ref[...] += part


def main_kernel(where_ref, gain_ref, stat_ref, seg_row_ref, seg_col_ref, qgain_ref, kgain_ref,
                cot_ref, part_ref, normed_ref, packed_hbm, *rest):
    n_early = len(EARLY)
    early_refs, late_refs = rest[:n_early], rest[n_early:n_early + NX]
    rest = rest[n_early + NX:]
    n_copies = (n_early + 1) * NX
    attn_ref, keep_a, keep_b, give_a, give_b = rest[:5]
    weight_ref, rows_ref, packed_ref, acc_ref, grad_ref, sems = rest[5:]
    zh, c = where_ref[1], where_ref[2]
    blocks = weight_blocks(where_ref)
    final = NZ * NX - len(LATE)

    arrived = load_weights(early_refs, late_refs, weight_ref, sems)
    last_copy = arrived.pop(final)
    last_copy.start()
    row_copies = [
        pltpu.make_async_copy(
            normed_ref.at[block_rows(blocks[final + j]), :], rows_ref.at[j], sems.at[n_copies + j])
        for j in range(len(LATE))
    ]
    packed_copy = pltpu.make_async_copy(packed_hbm, packed_ref, sems.at[n_copies + len(LATE)])
    for copy in row_copies + list(arrived.values()) + [packed_copy]:
        copy.start()

    last_copy.wait()
    for j, copy in enumerate(row_copies):
        copy.wait()
        part = contract(rows_ref[j], weight_ref[final + j], 0, 0)
        if j == 0:
            acc_ref[...] = part_ref[...] + part
        else:
            acc_ref[...] += part

    factor = 1.0 / math.sqrt(DH)
    same = seg_col_ref[...] == seg_row_ref[...]
    width = qgain_ref.shape[1]
    for h in range(width // DH):
        cols = slice(h * DH, (h + 1) * DH)
        qgain, kgain = qgain_ref[:, cols], kgain_ref[:, cols]
        query_hat, query_inv = row_norm(acc_ref[:, h * DH:(h + 1) * DH])
        key_hat, key_inv = row_norm(acc_ref[:, width + h * DH:width + (h + 1) * DH])
        value = acc_ref[:, 2 * width + h * DH:2 * width + (h + 1) * DH].astype(BF)
        query = (query_hat * qgain).astype(BF)
        key = (key_hat * kgain).astype(BF)
        cot = cot_ref[:, cols]
        scores = jnp.where(same, contract(query, key, 1, 1) * factor, NEGATIVE)
        exp_scores = jnp.exp(scores - jnp.max(scores, axis=-1, keepdims=True))
        prob = exp_scores / jnp.sum(exp_scores, axis=-1, keepdims=True)
        prob_half = prob.astype(BF)
        attn_ref[:, cols] = contract(prob_half, value, 1, 0).astype(BF)
        grad_prob = contract(cot, value, 1, 1)
        delta = jnp.sum(prob * grad_prob, axis=-1, keepdims=True)
        grad_score = (prob * (grad_prob - delta) * factor).astype(BF)
        query_side = contract(grad_score, key, 1, 0)
        key_side = contract(grad_score, query, 0, 0)
        grad_ref[:, h * DH:(h + 1) * DH] = norm_back(
            query_side * qgain, query_hat, query_inv).astype(BF)
        grad_ref[:, width + h * DH:width + (h + 1) * DH] = norm_back(
            key_side * kgain, key_hat, key_inv).astype(BF)
        grad_ref[:, 2 * width + h * DH:2 * width + (h + 1) * DH] = contract(
            prob_half, cot, 0, 0).astype(BF)

    mean, inverse = stat_ref[0:1, :], stat_ref[1:2, :]
    first = jnp.zeros((1, LEN), F32)
    second = jnp.zeros((1, LEN), F32)
    packed_copy.wait()
    for slot, block in enumerate(blocks):
        if slot in arrived:
            arrived[slot].wait()
        rows = block_rows(block)
        term = contract(weight_ref[slot], grad_ref[...], 1, 1).astype(BF)
        scaled = term.astype(F32) * gain_ref[rows, :]
        first = first + jnp.sum(scaled, axis=0, keepdims=True)
        second = second + jnp.sum(
            scaled * (packed_ref[rows, :].astype(F32) - mean), axis=0, keepdims=True)
        same_core = lax.rem(block // 2, NC) == c
        same_half = lax.rem(block // 4, NH) == zh
        target = (block // 8) * SHARD + lax.rem(block, 2) * BLOCK
        out = pl.ds(pl.multiple_of(target, BLOCK), BLOCK)
        for core_flag, half_flag, ref in (
            (True, True, keep_a), (True, False, keep_b),
            (False, True, give_a), (False, False, give_b),
        ):
            @pl.when(jnp.logical_and(same_core == core_flag, same_half == half_flag))
            def _(ref=ref):
                ref[out, :] = term

    sums = split_sums(first, second * inverse)
    keep_b[NY * SHARD:, :] = sums
    give_b[NY * SHARD:, :] = sums


def split_sums(first, second):
    rows = []
    for value in (first, second):
        for _ in range(3):
            piece = value.astype(BF)
            rows.append(piece.astype(F32))
            value = value - piece.astype(F32)
    rows.append(jnp.zeros((TAIL - len(rows), LEN), F32))
    return jnp.concatenate(rows, axis=0).astype(BF)


def join_sums(tail):
    tail = tail.astype(F32)
    return (
        tail[..., 0:1, :] + tail[..., 1:2, :] + tail[..., 2:3, :],
        tail[..., 3:4, :] + tail[..., 4:5, :] + tail[..., 5:6, :],
    )


def send_packets(patches, destination):
    rows = patches.shape[0]
    n_groups = NZ * NX
    owners = destination // LEN
    offsets = destination % LEN
    one_hot = (owners[:, None] == jnp.arange(n_groups)[None, :]).astype(BF)
    index = jnp.arange(rows)
    strict = (index[:, None] > index[None, :]).astype(BF)
    earlier = jnp.dot(strict, one_hot, preferred_element_type=F32)
    rank = jnp.sum(earlier * one_hot.astype(F32), axis=1).astype(jnp.int32)
    position = owners * CAP + rank
    placing = jnp.arange(n_groups * CAP)[:, None] == position[None, :]
    sent = jnp.dot(placing.astype(BF), patches, preferred_element_type=F32).astype(BF)
    places = jnp.sum(jnp.where(placing, offsets[None, :] + 1, 0), axis=1)
    places = places.reshape(n_groups, 1, CAP).astype(BF)
    places = jnp.pad(places, ((0, 0), (0, 7), (0, 128 - CAP)))
    blocks = [
        sent[:, i:i + 128].reshape(n_groups, CAP, 128) for i in range(0, sent.shape[1], 128)
    ]
    return jnp.concatenate(blocks + [places], axis=1)


def unpack(got):
    n_groups = got.shape[0]
    n_blocks = (got.shape[1] - 8) // CAP
    places = got[:, n_blocks * CAP, :CAP].astype(jnp.int32).reshape(n_groups * CAP) - 1
    chosen = (places[:, None] == jnp.arange(LEN)[None, :]).astype(BF)
    out = [
        contract(
            got[:, i * CAP:(i + 1) * CAP].reshape(n_groups * CAP, 128), chosen, 0, 0
        ).astype(BF)
        for i in range(n_blocks)
    ]
    return jnp.concatenate(out, axis=0)


def per_device(patches, destination, segment, ln_gain, w_query, w_key, w_value,
               query_gain, key_gain, attn_cotangent):
    y, zh, c = lax.axis_index("y"), lax.axis_index("zh"), lax.axis_index("c")
    zl, x = lax.axis_index("zl"), lax.axis_index("x")
    where = jnp.stack([y, zh, c, zl, x]).astype(jnp.int32)
    gain_column = ln_gain[:, None]

    weight = jnp.concatenate([w_query, w_key, w_value], axis=1)
    packets = send_packets(patches, destination)

    x_ring = functools.partial(lax.ppermute, axis_name=("x", "c"), perm=core_ring(NX))
    y_ring = functools.partial(lax.ppermute, axis_name=("y", "c"), perm=core_ring(NY))
    got = lax.all_to_all(packets, ("zl", "x"), split_axis=0, concat_axis=0, tiled=True)
    mine = unpack(got)
    partner = lax.ppermute(mine, "zh", shift(NH, 1))
    g = [jnp.stack([mine, partner])]
    g.append(y_ring(g[0]))
    wait_for = {2: got, 3: partner, 4: g[1]}
    z = {0: weight}
    for step in (1, 2, 3, 4):
        block = z[step - 1]
        if step in wait_for:
            block = after(block, wait_for[step])
        z[step] = lax.ppermute(block, "zl", Z_RING)
        if step < 4:
            z[-step] = lax.ppermute(z[1 - step], "zl", Z_BACK)
    early = []
    for steps in EARLY:
        joined = lax.all_gather(
            jnp.concatenate([after(z[n], partner) if n == -2 else z[n] for n in steps]),
            "x", axis=0, tiled=True)
        early.append(joined.reshape((NX, len(steps)) + weight.shape))
    for _ in range(NY - 2):
        g.append(y_ring(g[-1]))
    most = lax.ppermute(jnp.concatenate(g[:3]), "c", shift(NC, 1))
    last = lax.ppermute(g[3], "c", shift(NC, 1))

    held = after(after(z[-3], most), last)
    late = [jnp.stack([held if n == -3 else z[n] for n in LATE])]
    late.append(x_ring(late[0]))

    vmem = pl.BlockSpec(memory_space=pltpu.VMEM)
    smem = pl.BlockSpec(memory_space=pltpu.SMEM)
    normed, packed, stat = pl.pallas_call(
        norm_kernel,
        out_shape=(
            jax.ShapeDtypeStruct((D, LEN), BF),
            jax.ShapeDtypeStruct((D, LEN), BF),
            jax.ShapeDtypeStruct((2, LEN), F32),
        ),
        in_specs=[smem] + [vmem] * 7,
        out_specs=(vmem, vmem, vmem),
        compiler_params=pltpu.CompilerParams(vmem_limit_bytes=32 << 20),
        cost_estimate=pl.CostEstimate(flops=20_000_000, bytes_accessed=10_000_000, transcendentals=0),
        name="norm",
    )(where, gain_column, *g, most, last)

    late.append(x_ring(after(late[1], normed)))
    late.append(x_ring(late[2]))

    width = w_query.shape[1]
    hbm = pl.BlockSpec(memory_space=pl.ANY)
    n_first = NZ * NX - len(LATE)
    part = pl.pallas_call(
        first_kernel,
        out_shape=jax.ShapeDtypeStruct((LEN, 3 * width), F32),
        in_specs=[smem, vmem] + [hbm] * (len(EARLY) + NX - 1),
        out_specs=vmem,
        scratch_shapes=[
            pltpu.VMEM((n_first,) + weight.shape, BF),
            pltpu.SemaphoreType.DMA(((len(EARLY) + 1) * NX - 1,)),
        ],
        compiler_params=pltpu.CompilerParams(vmem_limit_bytes=54 << 20),
        cost_estimate=pl.CostEstimate(
            flops=2_200_000_000, bytes_accessed=12_000_000, transcendentals=0),
        name="first",
    )(where, normed, *early, *late[:NX - 1])

    half = jax.ShapeDtypeStruct((NY * SHARD, LEN), BF)
    half_tail = jax.ShapeDtypeStruct((NY * SHARD + TAIL, LEN), BF)
    context, keep_a, keep_b, give_a, give_b = pl.pallas_call(
        main_kernel,
        out_shape=(jax.ShapeDtypeStruct((LEN, width), BF), half, half_tail, half, half_tail),
        in_specs=[smem] + [vmem] * 8 + [hbm] * (2 + len(EARLY) + NX),
        out_specs=(vmem,) * 5,
        scratch_shapes=[
            pltpu.VMEM((NZ * NX,) + weight.shape, BF),
            pltpu.VMEM((len(LATE), BLOCK, LEN), BF),
            pltpu.VMEM((D, LEN), BF),
            pltpu.VMEM((LEN, 3 * width), F32),
            pltpu.VMEM((LEN, 3 * width), BF),
            pltpu.SemaphoreType.DMA(((len(EARLY) + 1) * NX + len(LATE) + 1,)),
        ],
        compiler_params=pltpu.CompilerParams(vmem_limit_bytes=36 << 20),
        cost_estimate=pl.CostEstimate(
            flops=3_000_000_000, bytes_accessed=20_000_000, transcendentals=131072),
        name="core",
    )(where, gain_column, stat, segment[None, :], segment[:, None], query_gain[None, :],
      key_gain[None, :], attn_cotangent, part, normed, packed, *early, *late)

    rows = NY * SHARD
    y_swap = functools.partial(
        lax.all_to_all, axis_name="y", split_axis=0, concat_axis=0, tiled=True)
    taken = lax.ppermute(give_b, "c", shift(NC, 1))
    tails = [a + b for a, b in zip(join_sums(keep_b[rows:]), join_sums(taken[rows:]))]
    both = (keep_b[:rows].astype(F32) + taken[:rows].astype(F32)).astype(BF)
    tail = jnp.broadcast_to(split_sums(*tails)[None], (NY, TAIL, LEN))
    got_b = y_swap(jnp.concatenate([both.reshape(NY, SHARD, LEN), tail], axis=1))
    taken = lax.ppermute(give_a, "c", shift(NC, 1))
    both = (keep_a.astype(F32) + taken.astype(F32)).astype(BF)
    got_a = y_swap(both.reshape(NY, SHARD, LEN))
    leave = jnp.sum(got_b[:, :SHARD].astype(F32), axis=0).astype(BF)
    sums = [jnp.sum(a, axis=0) for a in join_sums(got_b[:, SHARD:])]
    came = lax.ppermute(
        jnp.concatenate([leave, split_sums(*sums)], axis=0), "zh", shift(NH, 1))
    shard = jnp.sum(got_a.astype(F32), axis=0) + came[:SHARD].astype(F32)
    first, second = [a + b for a, b in zip(sums, join_sums(came[SHARD:]))]

    index = (y * NH + zh) * NC + c
    gain_here = lax.dynamic_slice_in_dim(ln_gain, index * SHARD, SHARD, 0)[:, None]
    mean, inverse = stat[0:1], stat[1:2]
    x_hat = (mine.astype(F32) - mean) * inverse
    grad = (shard * gain_here - first / D - x_hat * (second / D)) * inverse
    return context, grad.T.astype(BF)


def solution(mesh):
    fine = Mesh(mesh.devices.reshape(NZ, NX, NY, NH, NC), ("zl", "x", "y", "zh", "c"))
    dp, mp = ("zl", "x"), ("y", "zh", "c")
    placed = (
        P(dp, mp), P(dp), P(dp), P(), P(dp, mp), P(dp, mp), P(dp, mp), P(mp), P(mp), P(dp, mp),
    )
    return jax.shard_map(
        per_device,
        mesh=fine,
        in_specs=placed,
        out_specs=(P(dp, mp), P(dp, mp)),
        check_vma=False,
    )
```

```python
import functools
import math

import jax
import jax.numpy as jnp
from jax import lax
from jax.experimental import pallas as pl
from jax.experimental.pallas import tpu as pltpu
from jax.sharding import Mesh, PartitionSpec as P

D = 6144
DH = 128
LEN = 256
CAP = 16
NZ, NX, NY, NH, NC = 8, 4, 4, 2, 2
SHARD = D // (NY * NH * NC)
BLOCK = D // (NZ * NX)
EPSILON = 1e-06
NEGATIVE = -1e30
BF = jnp.bfloat16
F32 = jnp.float32
FOLD = [0, 2, 4, 6, 7, 5, 3, 1]
Z_RING = [(FOLD[i], FOLD[(i + 1) % NZ]) for i in range(NZ)]
Z_BACK = [(b, a) for a, b in Z_RING]
EARLY = ((0,), (1, -1), (2, -2))
LATE = (3, -3, 4)
TAIL = 16


def shift(n, k):
    return [(i, (i + k) % n) for i in range(n)]


def core_ring(n):
    return [(i * NC + k, (i + (1, n - 1)[k]) % n * NC + k) for i in range(n) for k in range(NC)]


def after(value, other):
    return value + other[(0,) * other.ndim] * 0


def contract(a, b, dim_a, dim_b):
    return lax.dot_general(
        a, b, (((dim_a,), (dim_b,)), ((), ())), preferred_element_type=F32
    )


def ring_source(place, core, steps, n):
    return lax.rem(place + jnp.where(core == 0, n - steps, steps), n)


def norm_kernel(where_ref, gain_ref, *rest):
    y, zh, c = where_ref[0], where_ref[1], where_ref[2]
    own, others = rest[:NY], rest[NY:NY + 2]
    normed_ref, packed_ref, stat_ref = rest[NY + 2:]
    blocks = []
    for steps in range(NY):
        for flip in range(NH):
            half = lax.rem(zh + flip, NH)
            there = ring_source(y, c, steps, NY) * NH + half
            blocks.append((own[steps], flip, there * NC + c))
            there = ring_source(y, 1 - c, steps, NY) * NH + half
            ref, i = (others[0], 2 * steps + flip) if steps < NY - 1 else (others[1], flip)
            blocks.append((ref, i, there * NC + (1 - c)))
    total = jnp.zeros((1, LEN), F32)
    for ref, i, _ in blocks:
        total = total + jnp.sum(ref[i].astype(F32), axis=0, keepdims=True)
    mean = total / D
    total = jnp.zeros((1, LEN), F32)
    for ref, i, _ in blocks:
        centred = ref[i].astype(F32) - mean
        total = total + jnp.sum(centred * centred, axis=0, keepdims=True)
    inverse = lax.rsqrt(total / D + EPSILON)
    stat_ref[0:1, :] = mean
    stat_ref[1:2, :] = inverse
    for ref, i, index in blocks:
        rows = pl.ds(pl.multiple_of(index * SHARD, SHARD), SHARD)
        value = ref[i]
        packed_ref[rows, :] = value
        normed_ref[rows, :] = (
            (value.astype(F32) - mean) * inverse * gain_ref[rows, :]
        ).astype(BF)


def row_norm(values_in):
    row_mean = jnp.mean(values_in, axis=-1, keepdims=True)
    centred = values_in - row_mean
    row_var = jnp.mean(centred * centred, axis=-1, keepdims=True)
    inverse = lax.rsqrt(row_var + EPSILON)
    return centred * inverse, inverse


def norm_back(grad_hat, scaled, inverse):
    first = jnp.mean(grad_hat, axis=-1, keepdims=True)
    second = jnp.mean(grad_hat * scaled, axis=-1, keepdims=True)
    return (grad_hat - first - scaled * second) * inverse


def weight_blocks(where_ref):
    c, zl, x = where_ref[2], where_ref[3], where_ref[4]
    position = jnp.where(lax.rem(zl, 2) == 0, zl // 2, 7 - zl // 2)
    found = []
    for steps in EARLY + (LATE,):
        for off in range(NX):
            x_from = ring_source(x, c, off, NX) if steps is LATE else off
            for step in steps:
                p = lax.rem(position - step + NZ, NZ)
                z_from = jnp.where(p < 4, 2 * p, 15 - 2 * p)
                found.append(z_from * NX + x_from)
    return found


def block_rows(block):
    return pl.ds(pl.multiple_of(block * BLOCK, BLOCK), BLOCK)


def load_weights(early_refs, late_refs, weight_ref, sems):
    sources = []
    for ref in early_refs:
        sources.extend((ref.at[off], ref.shape[1]) for off in range(NX))
    sources.extend((ref, ref.shape[0]) for ref in late_refs)
    copies = {}
    slot = 0
    for n, (source, size) in enumerate(sources):
        copies[slot] = pltpu.make_async_copy(
            source, weight_ref.at[slot:slot + size], sems.at[n])
        slot += size
    return copies


def first_kernel(where_ref, normed_ref, *rest):
    early_refs, late_refs = rest[:len(EARLY)], rest[len(EARLY):len(EARLY) + NX - 1]
    acc_ref, weight_ref, sems = rest[len(EARLY) + NX - 1:]
    blocks = weight_blocks(where_ref)
    copies = load_weights(early_refs, late_refs, weight_ref, sems)
    for copy in copies.values():
        copy.start()
    for slot in range(weight_ref.shape[0]):
        if slot in copies:
            copies[slot].wait()
        part = contract(normed_ref[block_rows(blocks[slot]), :], weight_ref[slot], 0, 0)
        if slot == 0:
            acc_ref[...] = part
        else:
            acc_ref[...] += part


def main_kernel(where_ref, gain_ref, stat_ref, seg_row_ref, seg_col_ref, qgain_ref, kgain_ref,
                cot_ref, part_ref, normed_ref, packed_hbm, *rest):
    n_early = len(EARLY)
    early_refs, late_refs = rest[:n_early], rest[n_early:n_early + NX]
    rest = rest[n_early + NX:]
    n_copies = (n_early + 1) * NX
    attn_ref, keep_a, keep_b, give_a, give_b = rest[:5]
    weight_ref, rows_ref, packed_ref, acc_ref, grad_ref, sems = rest[5:]
    zh, c = where_ref[1], where_ref[2]
    blocks = weight_blocks(where_ref)
    final = NZ * NX - len(LATE)

    arrived = load_weights(early_refs, late_refs, weight_ref, sems)
    last_copy = arrived.pop(final)
    last_copy.start()
    row_copies = [
        pltpu.make_async_copy(
            normed_ref.at[block_rows(blocks[final + j]), :], rows_ref.at[j], sems.at[n_copies + j])
        for j in range(len(LATE))
    ]
    packed_copy = pltpu.make_async_copy(packed_hbm, packed_ref, sems.at[n_copies + len(LATE)])
    for copy in row_copies + list(arrived.values()) + [packed_copy]:
        copy.start()

    last_copy.wait()
    for j, copy in enumerate(row_copies):
        copy.wait()
        part = contract(rows_ref[j], weight_ref[final + j], 0, 0)
        if j == 0:
            acc_ref[...] = part_ref[...] + part
        else:
            acc_ref[...] += part

    factor = 1.0 / math.sqrt(DH)
    same = seg_col_ref[...] == seg_row_ref[...]
    width = qgain_ref.shape[1]
    for h in range(width // DH):
        cols = slice(h * DH, (h + 1) * DH)
        qgain, kgain = qgain_ref[:, cols], kgain_ref[:, cols]
        query_hat, query_inv = row_norm(acc_ref[:, h * DH:(h + 1) * DH])
        key_hat, key_inv = row_norm(acc_ref[:, width + h * DH:width + (h + 1) * DH])
        value = acc_ref[:, 2 * width + h * DH:2 * width + (h + 1) * DH].astype(BF)
        query = (query_hat * qgain).astype(BF)
        key = (key_hat * kgain).astype(BF)
        cot = cot_ref[:, cols]
        scores = jnp.where(same, contract(query, key, 1, 1) * factor, NEGATIVE)
        exp_scores = jnp.exp(scores - jnp.max(scores, axis=-1, keepdims=True))
        prob = exp_scores / jnp.sum(exp_scores, axis=-1, keepdims=True)
        prob_half = prob.astype(BF)
        attn_ref[:, cols] = contract(prob_half, value, 1, 0).astype(BF)
        grad_prob = contract(cot, value, 1, 1)
        delta = jnp.sum(prob * grad_prob, axis=-1, keepdims=True)
        grad_score = (prob * (grad_prob - delta) * factor).astype(BF)
        query_side = contract(grad_score, key, 1, 0)
        key_side = contract(grad_score, query, 0, 0)
        grad_ref[:, h * DH:(h + 1) * DH] = norm_back(
            query_side * qgain, query_hat, query_inv).astype(BF)
        grad_ref[:, width + h * DH:width + (h + 1) * DH] = norm_back(
            key_side * kgain, key_hat, key_inv).astype(BF)
        grad_ref[:, 2 * width + h * DH:2 * width + (h + 1) * DH] = contract(
            prob_half, cot, 0, 0).astype(BF)

    mean, inverse = stat_ref[0:1, :], stat_ref[1:2, :]
    first = jnp.zeros((1, LEN), F32)
    second = jnp.zeros((1, LEN), F32)
    packed_copy.wait()
    for slot, block in enumerate(blocks):
        if slot in arrived:
            arrived[slot].wait()
        rows = block_rows(block)
        term = contract(weight_ref[slot], grad_ref[...], 1, 1).astype(BF)
        scaled = term.astype(F32) * gain_ref[rows, :]
        first = first + jnp.sum(scaled, axis=0, keepdims=True)
        second = second + jnp.sum(
            scaled * (packed_ref[rows, :].astype(F32) - mean), axis=0, keepdims=True)
        same_core = lax.rem(block // 2, NC) == c
        same_half = lax.rem(block // 4, NH) == zh
        target = (block // 8) * SHARD + lax.rem(block, 2) * BLOCK
        out = pl.ds(pl.multiple_of(target, BLOCK), BLOCK)
        for core_flag, half_flag, ref in (
            (True, True, keep_a), (True, False, keep_b),
            (False, True, give_a), (False, False, give_b),
        ):
            @pl.when(jnp.logical_and(same_core == core_flag, same_half == half_flag))
            def _(ref=ref):
                ref[out, :] = term

    sums = split_sums(first, second * inverse)
    keep_b[NY * SHARD:, :] = sums
    give_b[NY * SHARD:, :] = sums


def split_sums(first, second):
    rows = []
    for value in (first, second):
        for _ in range(3):
            piece = value.astype(BF)
            rows.append(piece.astype(F32))
            value = value - piece.astype(F32)
    rows.append(jnp.zeros((TAIL - len(rows), LEN), F32))
    return jnp.concatenate(rows, axis=0).astype(BF)


def join_sums(tail):
    tail = tail.astype(F32)
    return (
        tail[..., 0:1, :] + tail[..., 1:2, :] + tail[..., 2:3, :],
        tail[..., 3:4, :] + tail[..., 4:5, :] + tail[..., 5:6, :],
    )


def send_packets(patches, destination):
    rows = patches.shape[0]
    n_groups = NZ * NX
    owners = destination // LEN
    offsets = destination % LEN
    one_hot = (owners[:, None] == jnp.arange(n_groups)[None, :]).astype(BF)
    index = jnp.arange(rows)
    strict = (index[:, None] > index[None, :]).astype(BF)
    earlier = jnp.dot(strict, one_hot, preferred_element_type=F32)
    rank = jnp.sum(earlier * one_hot.astype(F32), axis=1).astype(jnp.int32)
    position = owners * CAP + rank
    placing = jnp.arange(n_groups * CAP)[:, None] == position[None, :]
    sent = jnp.dot(placing.astype(BF), patches, preferred_element_type=F32).astype(BF)
    places = jnp.sum(jnp.where(placing, offsets[None, :] + 1, 0), axis=1)
    places = places.reshape(n_groups, 1, CAP).astype(BF)
    places = jnp.pad(places, ((0, 0), (0, 7), (0, 128 - CAP)))
    blocks = [
        sent[:, i:i + 128].reshape(n_groups, CAP, 128) for i in range(0, sent.shape[1], 128)
    ]
    return jnp.concatenate(blocks + [places], axis=1)


def unpack(got):
    n_groups = got.shape[0]
    n_blocks = (got.shape[1] - 8) // CAP
    places = got[:, n_blocks * CAP, :CAP].astype(jnp.int32).reshape(n_groups * CAP) - 1
    chosen = (places[:, None] == jnp.arange(LEN)[None, :]).astype(BF)
    out = [
        contract(
            got[:, i * CAP:(i + 1) * CAP].reshape(n_groups * CAP, 128), chosen, 0, 0
        ).astype(BF)
        for i in range(n_blocks)
    ]
    return jnp.concatenate(out, axis=0)


def per_device(patches, destination, segment, ln_gain, w_query, w_key, w_value,
               query_gain, key_gain, attn_cotangent):
    y, zh, c = lax.axis_index("y"), lax.axis_index("zh"), lax.axis_index("c")
    zl, x = lax.axis_index("zl"), lax.axis_index("x")
    where = jnp.stack([y, zh, c, zl, x]).astype(jnp.int32)
    gain_column = ln_gain[:, None]

    weight = jnp.concatenate([w_query, w_key, w_value], axis=1)
    packets = send_packets(patches, destination)

    x_ring = functools.partial(lax.ppermute, axis_name=("x", "c"), perm=core_ring(NX))
    y_ring = functools.partial(lax.ppermute, axis_name=("y", "c"), perm=core_ring(NY))
    got = lax.all_to_all(packets, ("zl", "x"), split_axis=0, concat_axis=0, tiled=True)
    mine = unpack(got)
    z = {0: weight}
    for step in (1, 2):
        z[-step] = lax.ppermute(z[1 - step], "zl", Z_BACK)
    partner = lax.ppermute(after(mine, z[-2]), "zh", shift(NH, 1))
    g = [jnp.stack([mine, partner])]
    g.append(y_ring(g[0]))
    wait_for = {2: got, 3: partner, 4: g[1]}
    for step in (1, 2, 3, 4):
        block = z[step - 1]
        if step in wait_for:
            block = after(block, wait_for[step])
        z[step] = lax.ppermute(block, "zl", Z_RING)
        if step == 3:
            z[-step] = lax.ppermute(z[1 - step], "zl", Z_BACK)
    early = []
    for steps in EARLY:
        joined = lax.all_gather(
            jnp.concatenate([after(z[n], partner) if n == -2 else z[n] for n in steps]),
            "x", axis=0, tiled=True)
        early.append(joined.reshape((NX, len(steps)) + weight.shape))
    for _ in range(NY - 2):
        g.append(y_ring(g[-1]))
    late = [jnp.stack([after(z[n], g[3]) if n < 0 else z[n] for n in LATE])]
    for _ in range(NX - 2):
        late.append(x_ring(late[-1]))
    most = lax.ppermute(jnp.concatenate(g[:3]), "c", shift(NC, 1))
    last = lax.ppermute(g[3], "c", shift(NC, 1))

    vmem = pl.BlockSpec(memory_space=pltpu.VMEM)
    smem = pl.BlockSpec(memory_space=pltpu.SMEM)
    normed, packed, stat = pl.pallas_call(
        norm_kernel,
        out_shape=(
            jax.ShapeDtypeStruct((D, LEN), BF),
            jax.ShapeDtypeStruct((D, LEN), BF),
            jax.ShapeDtypeStruct((2, LEN), F32),
        ),
        in_specs=[smem] + [vmem] * 7,
        out_specs=(vmem, vmem, vmem),
        compiler_params=pltpu.CompilerParams(vmem_limit_bytes=32 << 20),
        cost_estimate=pl.CostEstimate(flops=20_000_000, bytes_accessed=10_000_000, transcendentals=0),
        name="norm",
    )(where, gain_column, *g, most, last)

    late.append(x_ring(after(late[2], normed)))

    width = w_query.shape[1]
    hbm = pl.BlockSpec(memory_space=pl.ANY)
    n_first = NZ * NX - len(LATE)
    part = pl.pallas_call(
        first_kernel,
        out_shape=jax.ShapeDtypeStruct((LEN, 3 * width), F32),
        in_specs=[smem, vmem] + [hbm] * (len(EARLY) + NX - 1),
        out_specs=vmem,
        scratch_shapes=[
            pltpu.VMEM((n_first,) + weight.shape, BF),
            pltpu.SemaphoreType.DMA(((len(EARLY) + 1) * NX - 1,)),
        ],
        compiler_params=pltpu.CompilerParams(vmem_limit_bytes=54 << 20),
        cost_estimate=pl.CostEstimate(
            flops=2_200_000_000, bytes_accessed=12_000_000, transcendentals=0),
        name="first",
    )(where, normed, *early, *late[:NX - 1])

    half = jax.ShapeDtypeStruct((NY * SHARD, LEN), BF)
    half_tail = jax.ShapeDtypeStruct((NY * SHARD + TAIL, LEN), BF)
    context, keep_a, keep_b, give_a, give_b = pl.pallas_call(
        main_kernel,
        out_shape=(jax.ShapeDtypeStruct((LEN, width), BF), half, half_tail, half, half_tail),
        in_specs=[smem] + [vmem] * 8 + [hbm] * (2 + len(EARLY) + NX),
        out_specs=(vmem,) * 5,
        scratch_shapes=[
            pltpu.VMEM((NZ * NX,) + weight.shape, BF),
            pltpu.VMEM((len(LATE), BLOCK, LEN), BF),
            pltpu.VMEM((D, LEN), BF),
            pltpu.VMEM((LEN, 3 * width), F32),
            pltpu.VMEM((LEN, 3 * width), BF),
            pltpu.SemaphoreType.DMA(((len(EARLY) + 1) * NX + len(LATE) + 1,)),
        ],
        compiler_params=pltpu.CompilerParams(vmem_limit_bytes=36 << 20),
        cost_estimate=pl.CostEstimate(
            flops=3_000_000_000, bytes_accessed=20_000_000, transcendentals=131072),
        name="core",
    )(where, gain_column, stat, segment[None, :], segment[:, None], query_gain[None, :],
      key_gain[None, :], attn_cotangent, part, normed, packed, *early, *late)

    rows = NY * SHARD
    y_swap = functools.partial(
        lax.all_to_all, axis_name="y", split_axis=0, concat_axis=0, tiled=True)
    taken = lax.ppermute(give_b, "c", shift(NC, 1))
    tails = [a + b for a, b in zip(join_sums(keep_b[rows:]), join_sums(taken[rows:]))]
    both = (keep_b[:rows].astype(F32) + taken[:rows].astype(F32)).astype(BF)
    tail = jnp.broadcast_to(split_sums(*tails)[None], (NY, TAIL, LEN))
    got_b = y_swap(jnp.concatenate([both.reshape(NY, SHARD, LEN), tail], axis=1))
    taken = lax.ppermute(give_a, "c", shift(NC, 1))
    both = (keep_a.astype(F32) + taken.astype(F32)).astype(BF)
    got_a = y_swap(both.reshape(NY, SHARD, LEN))
    leave = jnp.sum(got_b[:, :SHARD].astype(F32), axis=0).astype(BF)
    sums = [jnp.sum(a, axis=0) for a in join_sums(got_b[:, SHARD:])]
    came = lax.ppermute(
        jnp.concatenate([leave, split_sums(*sums)], axis=0), "zh", shift(NH, 1))
    shard = jnp.sum(got_a.astype(F32), axis=0) + came[:SHARD].astype(F32)
    first, second = [a + b for a, b in zip(sums, join_sums(came[SHARD:]))]

    index = (y * NH + zh) * NC + c
    gain_here = lax.dynamic_slice_in_dim(ln_gain, index * SHARD, SHARD, 0)[:, None]
    mean, inverse = stat[0:1], stat[1:2]
    x_hat = (mine.astype(F32) - mean) * inverse
    grad = (shard * gain_here - first / D - x_hat * (second / D)) * inverse
    return context, grad.T.astype(BF)


def solution(mesh):
    fine = Mesh(mesh.devices.reshape(NZ, NX, NY, NH, NC), ("zl", "x", "y", "zh", "c"))
    dp, mp = ("zl", "x"), ("y", "zh", "c")
    placed = (
        P(dp, mp), P(dp), P(dp), P(), P(dp, mp), P(dp, mp), P(dp, mp), P(mp), P(mp), P(dp, mp),
    )
    return jax.shard_map(
        per_device,
        mesh=fine,
        in_specs=placed,
        out_specs=(P(dp, mp), P(dp, mp)),
        check_vma=False,
    )
```
